256 devices in a mesh: frame: 16 (over z, core), tok: 16 (over x, y).
Axes of the slice: x: 4, y: 4, z: 8, core: 2. Of those that a mesh axis runs over, the one named last changes fastest.
Arguments:
- stream: bfloat16 [16, 4096, 1152], P('frame', 'tok'), may hold values from -20 to 20
- queries: bfloat16 [16, 4096, 1152], P('frame', 'tok'), may hold values from -200 to 200
- key_vectors: bfloat16 [16, 4096, 1152], P('frame', 'tok'), may hold values from -6 to 6
- value_vectors: bfloat16 [16, 4096, 1152], P('frame', 'tok'), may hold values from -6 to 6
- modulation: float32 [16, 4, 1152], P('frame'), may hold values from -4 to 4
- output_weight: bfloat16 [1152, 1152], replicated, may hold values from -0.1875 to 0.1875
- output_bias: float32 [1152], replicated, may hold values from -3 to 3
- router_weight: bfloat16 [1152, 16], replicated, may hold values from -0.1875 to 0.1875
- expand_weight: bfloat16 [16, 1152, 4608], P('frame', None, 'tok'), may hold values from -0.1875 to 0.1875
- expand_bias: float32 [16, 4608], P('frame', 'tok'), may hold values from -3 to 3
- reduce_weight: bfloat16 [16, 4608, 1152], P('frame', 'tok'), may hold values from -0.09375 to 0.09375
- reduce_bias: float32 [16, 1152], P('frame'), may hold values from -3 to 3
- counts: int32 [16, 16], P(None, 'frame'), may hold values from 1 to 48, 256 in all within a row
- picked_rows: int32 [16, 16, 48], P(None, 'frame'), may hold values from 0 to 4095, as said below
Outputs:
- layer_out: bfloat16 [16, 4096, 1152], P('frame', 'tok')
The draws below stay inside these ranges and needn't reach their ends.
Inputs may be any that keep to these rules, and one draw needn't show every extreme that they name: counts[e, g] slots of block (e, g) are used; the counts of one expert sum to 256. The entries of one block picked_rows[e, g, :] are distinct positions among the 4096 tokens of frame g; slots at or beyond counts[e, g] are unused.
All inputs are finite; a program needn't handle non-finite values.
Results may differ from the reference program's by a relative error of at most 0.0055.
Values may be sent and summed in bfloat16 or wider, within the bound.
No kernel may reach another device: no remote copies, remote signals or barrier semaphores. Data moves between devices by JAX's collectives and lax.ppermute only.
A program may use at most 64 MiB of HBM per device.

```python
import math
import jax
import jax.numpy as jnp
import numpy as np
from jax import lax

D = 1152
H = 16
HD = 72
FF = 4608
CAP = 256
FTOK = 4096
FRAMES = 16
EXPERTS = 16
BLK = 48
N_FRAME = 16


def draw_stream(key, part):
    first_key, second_key = jax.random.split(key, 2)
    column_scale = jnp.exp(jax.random.uniform(second_key, (1, 1, D), jnp.float32, math.log(0.3), math.log(3.0)))
    values = jax.random.normal(first_key, (FRAMES, FTOK, D), jnp.float32) * column_scale
    return jnp.clip(values, -20.0, 20.0).astype(jnp.bfloat16)


def drawn_pair(key):
    key_draw = jnp.clip(jax.random.normal(jax.random.fold_in(key, 17), (FRAMES, FTOK, D), jnp.float32), -6.0, 6.0)
    query_draw = jnp.clip(2.5 * jax.random.normal(jax.random.fold_in(key, 29), (FRAMES, FTOK, D), jnp.float32), -15.0, 15.0)
    return (query_draw, key_draw)


def draw_queries(key, part):
    query_draw, key_draw = drawn_pair(key)
    return query_draw.astype(jnp.bfloat16)


def draw_key_vectors(key, part):
    query_draw, key_draw = drawn_pair(key)
    return key_draw.astype(jnp.bfloat16)


def draw_picked_rows(key, part):
    block_keys = jax.random.split(key, EXPERTS * N_FRAME)

    def one_block(block_key):
        return jax.random.permutation(block_key, FTOK)[:BLK].astype(jnp.int32)
    picked = jax.vmap(one_block)(block_keys).reshape(EXPERTS, N_FRAME, BLK)
    upper = (picked[0, 0] - picked[0, 0, 0] + FTOK - 1) % FTOK
    lower = (picked[0, 1] - picked[0, 1, 0]) % FTOK
    picked = picked.at[0, 0].set(upper.astype(jnp.int32))
    picked = picked.at[0, 1].set(lower.astype(jnp.int32))
    return picked.astype(jnp.int32)


def block_levels(own_key, shape, shards, least, high):
    def one(axis_at, shards_of):
        steps = jax.random.uniform(jax.random.fold_in(jax.random.fold_in(own_key, 6), axis_at), (shards_of,), jnp.float32, least / len(shards), high / len(shards))
        return jnp.repeat(jnp.exp(steps), shape[axis_at] // shards_of).reshape((-1,) + (1,) * (len(shape) - axis_at - 1))

    level = one(*shards[0])
    for cut in shards[1:]:
        level = level * one(*cut)
    return level


def split_up(count, total, bound, slope):
    portions = [(1 << 20) // math.isqrt(rank ** slope) + 1 for rank in range(2, count + 1)]
    rest, given = total - bound - (count - 1), [1] * (count - 1)
    while rest > 0:
        free = [i for i in range(count - 1) if given[i] < bound]
        whole, budget = sum([portions[i] for i in free]), rest
        for i in free:
            more = min(bound - given[i], max(1, budget * portions[i] // whole), rest)
            given[i] = given[i] + more
            rest = rest - more
    return np.array([bound] + given)


def ragged_sizes(own_key, number_of, total, most, lean):
    if number_of == 2:
        one = jax.random.randint(own_key, (), max(1, total - most), min(most, total - 1) + 1)
        return jnp.stack([one, total - one])
    lengths = jnp.asarray(split_up(number_of, total, most, lean), jnp.int32)
    twos = (number_of - 1) // 2
    donor, receiver = lengths[1:1 + 2 * twos:2], lengths[2:2 + 2 * twos:2]
    room = jnp.minimum(donor - 1, most - receiver)
    passed = jax.random.randint(jax.random.fold_in(own_key, 1), (twos,), 0, 1 << 20) % (room + 1)
    lengths = lengths.at[1:1 + 2 * twos:2].set(donor - passed).at[2:2 + 2 * twos:2].set(receiver + passed)
    return lengths[jax.random.permutation(jax.random.fold_in(own_key, 2), number_of)]


def noise(own_key, shape, spread, most, cuts=(), kind=jnp.bfloat16):
    array = spread * jax.random.normal(own_key, shape, jnp.float32)
    if cuts:
        array = array * block_levels(own_key, shape, cuts, -0.22, 0.18)
    return jnp.clip(array, -most, most).astype(kind)


def setup_inputs(seed: int = 0) -> dict:
    keys = jax.random.split(jax.random.key(seed), 15)
    stream = draw_stream(jax.random.fold_in(keys[14], 71), 0)
    queries = draw_queries(jax.random.fold_in(keys[14], 71), 0)
    key_vectors = draw_key_vectors(jax.random.fold_in(keys[14], 71), 0)
    value_vectors = noise(keys[3], (FRAMES, FTOK, D), 1.0, 6.0, ((0, 16), (1, 16)))
    modulation = noise(keys[4], (FRAMES, 4, D), 1.0, 4.0, ((0, 16),), jnp.float32)
    output_weight = noise(keys[5], (D, D), D ** -0.5, 0.1875)
    output_bias = noise(keys[6], (D,), 0.5, 3.0, (), jnp.float32)
    router_weight = noise(keys[7], (D, EXPERTS), D ** -0.5, 0.1875)
    expand_weight = noise(keys[8], (EXPERTS, D, FF), D ** -0.5, 0.1875, ((0, 16), (2, 16)))
    expand_bias = noise(keys[9], (EXPERTS, FF), 0.5, 3.0, ((0, 16), (1, 16)), jnp.float32)
    reduce_weight = noise(keys[10], (EXPERTS, FF, D), FF ** -0.5, 0.09375, ((0, 16), (1, 16)))
    reduce_bias = noise(keys[11], (EXPERTS, D), 0.5, 3.0, ((0, 16),), jnp.float32)
    counts = jax.vmap(lambda own: ragged_sizes(own, N_FRAME, CAP, BLK, 2))(jax.random.split(keys[12], EXPERTS)).reshape((EXPERTS, N_FRAME)).astype(jnp.int32)
    picked_rows = draw_picked_rows(jax.random.fold_in(keys[14], 71), 0)
    return {"stream": stream, "queries": queries, "key_vectors": key_vectors, "value_vectors": value_vectors, "modulation": modulation, "output_weight": output_weight, "output_bias": output_bias, "router_weight": router_weight, "expand_weight": expand_weight, "expand_bias": expand_bias, "reduce_weight": reduce_weight, "reduce_bias": reduce_bias, "counts": counts, "picked_rows": picked_rows}


def layer_norm(values):
    mean_val = lax.optimization_barrier(jnp.mean(values, axis=-1, keepdims=True))
    centred = values - mean_val
    variance = lax.optimization_barrier(jnp.mean(centred * centred, axis=-1, keepdims=True))
    return centred * lax.rsqrt(variance + 1e-06)

def head_attention(operands):
    head_queries, head_keys, head_values = operands
    scores = jnp.dot(head_queries, head_keys.T, preferred_element_type=jnp.float32) * (1.0 / math.sqrt(HD))
    scores = scores - lax.optimization_barrier(jnp.max(scores, axis=-1, keepdims=True))
    exponent = jnp.exp(scores)
    weights = (exponent / lax.optimization_barrier(jnp.sum(exponent, axis=-1, keepdims=True))).astype(jnp.bfloat16)
    return jnp.dot(weights, head_values, preferred_element_type=jnp.float32).astype(jnp.bfloat16)

def split_heads(tensor):
    return tensor.reshape(FRAMES, FTOK, H, HD).transpose(0, 2, 1, 3).reshape(FRAMES * H, FTOK, HD)

def reference(stream, queries, key_vectors, value_vectors, modulation, output_weight, output_bias, router_weight, expand_weight, expand_bias, reduce_weight, reduce_bias, counts, picked_rows):
    attended = lax.map(head_attention, (split_heads(queries), split_heads(key_vectors), split_heads(value_vectors)))
    attended = attended.reshape(FRAMES, H, FTOK, HD).transpose(0, 2, 1, 3).reshape(FRAMES * FTOK, D)
    projected = jnp.dot(attended, output_weight, preferred_element_type=jnp.float32) + output_bias
    projected = projected.reshape(FRAMES, FTOK, D)
    residual = (stream.astype(jnp.float32) + modulation[:, 0:1, :] * projected).astype(jnp.bfloat16)
    normed = layer_norm(residual.astype(jnp.float32)) * (1.0 + modulation[:, 2:3, :]) + modulation[:, 1:2, :]
    normed = normed.astype(jnp.bfloat16)
    gate_values = jax.nn.sigmoid(jnp.dot(normed.reshape(FRAMES * FTOK, D), router_weight, preferred_element_type=jnp.float32)).reshape(FRAMES, FTOK, EXPERTS)
    slot_ids = jnp.arange(BLK, dtype=jnp.int32)
    in_use_all = slot_ids[None, None, :] < counts[:, :, None]
    frame_ids = jnp.arange(FRAMES, dtype=jnp.int32)[:, None]

    def one_expert(total, operands):
        expert_id, row_index, in_use, expand_one, expand_bias_one, reduce_one, reduce_bias_one = operands
        chosen = normed[frame_ids, row_index]
        chosen = jnp.where(in_use[:, :, None], chosen, jnp.zeros_like(chosen)).reshape(FRAMES * BLK, D)
        hidden = jax.nn.gelu(jnp.dot(chosen, expand_one, preferred_element_type=jnp.float32) + expand_bias_one, approximate=True).astype(jnp.bfloat16)
        expert_out = (jnp.dot(hidden, reduce_one, preferred_element_type=jnp.float32) + reduce_bias_one).astype(jnp.bfloat16)
        mix_weight = gate_values[frame_ids, row_index, expert_id]
        mix_weight = jnp.where(in_use, mix_weight, jnp.zeros_like(mix_weight)).astype(jnp.bfloat16)
        term = mix_weight.astype(jnp.float32)[:, :, None] * expert_out.reshape(FRAMES, BLK, D).astype(jnp.float32)
        total = total.at[frame_ids, row_index].add(term)
        return (total, None)
    expert_ids = jnp.arange(EXPERTS, dtype=jnp.int32)
    expert_mix, unused = lax.scan(one_expert, jnp.zeros((FRAMES, FTOK, D), jnp.float32), (expert_ids, picked_rows, in_use_all, expand_weight, expand_bias, reduce_weight, reduce_bias))
    return (residual.astype(jnp.float32) + modulation[:, 3:4, :] * expert_mix).astype(jnp.bfloat16)
```

```python
import functools
import math

import jax
import jax.numpy as jnp
from jax import lax
from jax.experimental import pallas as pl
from jax.experimental.pallas import tpu as pltpu
from jax.sharding import PartitionSpec as P

H = 16
HD = 72
D = 1152
TL = 256
F32 = jnp.float32
BF16 = jnp.bfloat16
EXP_SCALE = math.log2(math.e) / math.sqrt(HD)
PARAMS = pltpu.CompilerParams(vmem_limit_bytes=56 * 1024 * 1024)


def nt(left, right):
    return lax.dot_general(left, right, (((1,), (1,)), ((), ())), preferred_element_type=F32)


def nn(left, right):
    return jnp.dot(left, right, preferred_element_type=F32)


def eye(size):
    rows = lax.broadcasted_iota(jnp.int32, (size, size), 0)
    cols = lax.broadcasted_iota(jnp.int32, (size, size), 1)
    return (rows == cols).astype(F32).astype(BF16)


def one_hot(index, width, first=0):
    lanes = lax.broadcasted_iota(jnp.int32, (index.shape[0], width), 1)
    return (lanes == index - first).astype(F32).astype(BF16)


TILES = [(w * 256, min(256, D - w * 256)) for w in range(5)]


def split_kernel(k_ref, v_ref, q_ref, s_ref, out_ref):
    for i, ref in enumerate((k_ref, v_ref, q_ref, s_ref)):
        for start, size in TILES:
            turned = nt(eye(size), ref[:, start : start + size])
            for h in range(H):
                low, high = max(h * HD, start), min((h + 1) * HD, start + size)
                if low < high:
                    out_ref[h, i * HD + low - h * HD : i * HD + high - h * HD, :] = turned[
                        low - start : high - start
                    ].astype(BF16)


def fill_values(r_ref, v_ref):
    for j in range(16):
        v_ref[j, :HD, :] = r_ref[j, HD : 2 * HD, :]
        v_ref[j, HD:, :] = jnp.ones((8, TL), BF16)


def attend(q, r_ref, v_ref, s_ref):
    top = None
    for j in range(16):
        scores = nn(q, r_ref[j, :HD, :])
        s_ref[:, j * TL : (j + 1) * TL] = scores
        part = jnp.maximum(scores[:, :128], scores[:, 128:])
        top = part if top is None else jnp.maximum(top, part)
    top = jnp.max(top, axis=1, keepdims=True)
    total = None
    for j in range(16):
        weights = jnp.exp2((s_ref[:, j * TL : (j + 1) * TL] - top) * EXP_SCALE).astype(BF16)
        part = nt(weights, v_ref[j])
        total = part if total is None else total + part
    return total[:, :HD] / total[:, HD : HD + 1]


def picked_kernel(idx_ref, r_ref, out_ref, v_ref, s_ref):
    @pl.when(pl.program_id(0) == 0)
    def _():
        fill_values(r_ref, v_ref)

    index = idx_ref[...]
    rows = None
    for j in range(16):
        part = nt(one_hot(index, TL, j * TL), r_ref[j, 2 * HD :, :])
        rows = part if rows is None else rows + part
    out_ref[:, :HD] = attend(rows[:, :HD].astype(BF16), r_ref, v_ref, s_ref).astype(BF16)
    out_ref[:, HD:] = rows[:, HD:].astype(BF16)


def main_kernel(first, r_ref, out_ref, v_ref, s_ref):
    @pl.when(pl.program_id(0) == 0)
    def _():
        fill_values(r_ref, v_ref)

    q = nt(eye(TL), r_ref[first + pl.program_id(0), 2 * HD : 3 * HD, :]).astype(BF16)
    out = attend(q, r_ref, v_ref, s_ref).astype(BF16)
    out_ref[0] = nt(eye(HD), out).astype(BF16)


def attention(kernel, steps, ins, in_specs, out_shape, out_spec, name):
    whole = pl.BlockSpec((16, 4 * HD, TL), lambda i: (0, 0, 0))
    return pl.pallas_call(
        kernel,
        grid=(steps,),
        in_specs=in_specs + [whole],
        out_specs=out_spec,
        out_shape=jax.ShapeDtypeStruct(out_shape, BF16),
        scratch_shapes=[pltpu.VMEM((16, 80, TL), BF16), pltpu.VMEM((TL, 4096), F32)],
        compiler_params=PARAMS,
        cost_estimate=pl.CostEstimate(
            flops=steps * 4 * 256 * 4096 * 256, transcendentals=steps * 256 * 4096, bytes_accessed=2 << 20
        ),
        name=name,
    )(*ins)


def normed_kernel(x_ref, w_ref, b_ref, mod_ref, out_ref, att_ref, str_ref):
    for h in range(H):
        att_ref[:, h * HD : (h + 1) * HD] = x_ref[h, :, :HD].astype(F32)
        str_ref[:, h * HD : (h + 1) * HD] = x_ref[h, :, HD:].astype(F32)
    projected = nn(att_ref[...].astype(BF16), w_ref[...]) + b_ref[...]
    residual = (str_ref[...] + mod_ref[0:1, :] * projected).astype(BF16).astype(F32)
    centred = residual - jnp.mean(residual, axis=1, keepdims=True)
    variance = jnp.mean(centred * centred, axis=1, keepdims=True)
    normed = centred * lax.rsqrt(variance + 1e-06) * (1.0 + mod_ref[2:3, :]) + mod_ref[1:2, :]
    att_ref[...] = normed
    for e in range(16):
        out_ref[e] = att_ref[3 * e : 3 * e + 3, :].astype(BF16)


def compact_kernel(x_ref, idx_ref, out_ref, rows_ref):
    for g in range(16):
        rows_ref[3 * g : 3 * g + 3, :] = x_ref[g].astype(F32)
    lines = lax.broadcasted_iota(jnp.int32, (16, 48), 0)
    table = (lines == idx_ref[...]).astype(F32).astype(BF16)
    rows = nn(table, rows_ref[...].astype(BF16)).astype(BF16)
    for t in range(16):
        out_ref[t] = rows


def expert_kernel(x_ref, we_ref, be_ref, wr_ref, router_ref, out_ref, gate_ref):
    rows = x_ref[...]
    hidden = jax.nn.gelu(nn(rows, we_ref[...]) + be_ref[...], approximate=True).astype(BF16)
    for c in range(16):
        out_ref[c] = nt(wr_ref[c], hidden).astype(BF16)
    gate_ref[...] = jax.nn.sigmoid(nt(router_ref[...], rows)).astype(BF16).astype(F32)


def gather_kernel(x_ref, gate_ref, rb_ref, idx_ref, out_ref):
    total = x_ref[0, :HD, :].astype(F32)
    for t in range(1, 16):
        total = total + x_ref[t, :HD, :].astype(F32)
    rows = (total + rb_ref[...]).astype(BF16).astype(F32)
    rows = (rows * gate_ref[0:1, :]).astype(BF16)
    for i in range(3):
        index = idx_ref[i * 256 : (i + 1) * 256, :]
        out_ref[i * 256 : (i + 1) * 256, :] = nt(one_hot(index, 256), rows).astype(BF16)


def scatter_kernel(p_ref, idx_ref, out_ref):
    turned = nt(eye(HD), p_ref[...]).astype(BF16)
    index = idx_ref[...]
    for t in range(16):
        out_ref[t] = nn(turned, one_hot(index, TL, t * TL)).astype(BF16)


def residual_kernel(o_ref, s_ref, w_ref, b_ref, mod_ref, out_ref, att_ref):
    for h in range(H):
        att_ref[h * HD : (h + 1) * HD, :] = o_ref[h, HD:, :]
    projected = None
    for start, size in TILES:
        rows = nt(eye(TL), att_ref[start : start + size, :]).astype(BF16)
        part = nn(rows, w_ref[start : start + size, :])
        projected = part if projected is None else projected + part
    projected = projected + b_ref[...]
    out_ref[...] = (s_ref[...].astype(F32) + mod_ref[0:1, :] * projected).astype(BF16)


def final_kernel(m_ref, res_ref, mod_ref, out_ref, mix_ref):
    for c in range(16):
        mix_ref[c * HD : (c + 1) * HD, :] = m_ref[c]
    for start, size in TILES:
        cols = slice(start, start + size)
        mixed = nt(eye(TL), mix_ref[cols, :])
        out_ref[:, cols] = (
            res_ref[:, cols].astype(F32) + mod_ref[3:4, cols] * mixed
        ).astype(BF16)


def call(kernel, out_shape, name, scratch=()):
    return pl.pallas_call(
        kernel, out_shape=out_shape, scratch_shapes=list(scratch), compiler_params=PARAMS, name=name
    )


def shaped(*shape, dtype=BF16):
    return jax.ShapeDtypeStruct(shape, dtype)


def per_device(
    stream,
    queries,
    key_vectors,
    value_vectors,
    modulation,
    output_weight,
    output_bias,
    router_weight,
    expand_weight,
    expand_bias,
    reduce_weight,
    reduce_bias,
    counts,
    picked_rows,
):
    me_frame = lax.axis_index("frame").astype(jnp.int32)
    me_tok = lax.axis_index("tok").astype(jnp.int32)
    exchange = functools.partial(lax.all_to_all, split_axis=0, concat_axis=0, tiled=True)
    mod = modulation[0]
    out_bias = output_bias[None, :]

    sent = call(split_kernel, shaped(16, 4 * HD, TL), "split")(
        key_vectors[0], value_vectors[0], queries[0], stream[0]
    )
    heads = exchange(sent, "tok")

    own_counts = counts[:, 0]
    all_counts = lax.all_gather(own_counts, "frame", axis=1)
    frames = jnp.arange(16, dtype=jnp.int32)
    before = (frames[:, None] < frames[None, :]).astype(jnp.int32)
    offsets = jnp.sum(all_counts[:, :, None] * before[None, :, :], axis=1)
    is_own = (frames == me_frame).astype(jnp.int32)
    own_offsets = jnp.sum(offsets * is_own[None, :], axis=1)
    expert_offsets = jnp.sum(offsets * is_own[:, None], axis=0)
    expert_counts = jnp.sum(all_counts * is_own[:, None], axis=0)
    picked = picked_rows[:, 0, :]
    slots = jnp.arange(48, dtype=jnp.int32)
    thirds = jnp.arange(3, dtype=jnp.int32) * 16
    pick_slot = ((frames[:, None] - own_offsets[None, :]) & 15)[:, :, None] + thirds
    pick_pos = jnp.sum(
        jnp.where(pick_slot[:, :, :, None] == slots, picked[None, :, None, :], 0), axis=3
    )
    pick_index = jnp.where(pick_slot < own_counts[None, :, None], pick_pos, -1).reshape(768, 1)
    held_slot = ((me_tok - expert_offsets) & 15)[:, None] + thirds
    held_index = jnp.where(
        held_slot < expert_counts[:, None], (expert_offsets[:, None] + held_slot) >> 4, -1
    ).reshape(1, 48)
    row_id = expert_offsets[:, None] + slots[None, :]
    back_index = jnp.where(
        slots[None, :] < expert_counts[:, None], (row_id & 15) * 16 + (row_id >> 4), -1
    ).reshape(768, 1)
    spread_index = jnp.where(slots[None, :] < own_counts[:, None], picked, -1).reshape(768, 1)

    router_own = jnp.sum(
        jnp.where((frames == me_frame)[None, :], router_weight, jnp.zeros_like(router_weight)), axis=1
    )
    router_rows = jnp.broadcast_to(router_own[None, :], (8, D))
    bias_own = lax.dynamic_slice_in_dim(reduce_bias[0].reshape(16, HD), me_tok, 1, 0).reshape(HD, 1)
    reduce_turned = reduce_weight[0].T.reshape(16, HD, 288)

    picked_out = attention(
        picked_kernel,
        3,
        (pick_index, heads),
        [pl.BlockSpec((TL, 1), lambda i: (i, 0))],
        (768, 2 * HD),
        pl.BlockSpec((TL, 2 * HD), lambda i: (i, 0)),
        "picked_attention",
    )
    heads, picked_out = lax.optimization_barrier((heads, picked_out))

    def main_part(first, steps):
        return attention(
            functools.partial(main_kernel, first),
            steps,
            (heads,),
            [],
            (steps, HD, TL),
            pl.BlockSpec((1, HD, TL), lambda i: (i, 0, 0)),
            "main_attention",
        )

    rows = exchange(picked_out.reshape(16, 48, 2 * HD), "tok")
    part_a = main_part(0, 5)
    rows, part_a = lax.optimization_barrier((rows, part_a))
    normed = call(
        normed_kernel, shaped(16, 3, D), "normed", [pltpu.VMEM((48, D), F32), pltpu.VMEM((48, D), F32)]
    )(rows, output_weight, out_bias, mod)
    normed = exchange(normed, "frame")
    part_b = main_part(5, 6)
    normed, part_b = lax.optimization_barrier((normed, part_b))
    rows = call(compact_kernel, shaped(16, 16, D), "compact", [pltpu.VMEM((48, D), F32)])(
        normed, held_index
    )
    rows = exchange(rows, "tok")
    part_c = main_part(11, 5)
    rows, part_c = lax.optimization_barrier((rows, part_c))
    partial_out, gates = call(
        expert_kernel, (shaped(16, HD, TL), shaped(8, TL, dtype=F32)), "expert"
    )(rows.reshape(TL, D), expand_weight[0], expand_bias, reduce_turned, router_rows)
    attended = jnp.concatenate([part_a, part_b, part_c], axis=0)
    both = exchange(jnp.concatenate([partial_out, attended], axis=1), "tok")
    outs = call(gather_kernel, shaped(768, HD), "weighted")(both, gates, bias_own, back_index)
    outs = exchange(outs.reshape(16, 48, HD), "frame")
    residual = call(residual_kernel, shaped(TL, D), "residual", [pltpu.VMEM((D, TL), BF16)])(
        both, stream[0], output_weight, out_bias, mod
    )
    mixed = call(scatter_kernel, shaped(16, HD, TL), "scatter")(outs.reshape(768, HD), spread_index)
    mixed = exchange(mixed, "tok")
    layer_out = call(final_kernel, shaped(TL, D), "final", [pltpu.VMEM((D, TL), BF16)])(
        mixed, residual, mod
    )
    return layer_out[None]


def solution(mesh):
    return jax.shard_map(
        per_device,
        mesh=mesh,
        in_specs=(
            P("frame", "tok", None),
            P("frame", "tok", None),
            P("frame", "tok", None),
            P("frame", "tok", None),
            P("frame", None, None),
            P(),
            P(),
            P(),
            P("frame", None, "tok"),
            P("frame", "tok"),
            P("frame", "tok", None),
            P("frame", None),
            P(None, "frame"),
            P(None, "frame", None),
        ),
        out_specs=P("frame", "tok", None),
        check_vma=False,
    )
```

```python
import functools
import math

import jax
import jax.numpy as jnp
from jax import lax
from jax.experimental import pallas as pl
from jax.experimental.pallas import tpu as pltpu
from jax.sharding import PartitionSpec as P

H = 16
HD = 72
D = 1152
TL = 256
F32 = jnp.float32
BF16 = jnp.bfloat16
SCALE = 1.0 / math.sqrt(HD)


def nt(left, right):
    return lax.dot_general(left, right, (((1,), (1,)), ((), ())), preferred_element_type=F32)


def nn(left, right):
    return jnp.dot(left, right, preferred_element_type=F32)


def eye(size):
    rows = lax.broadcasted_iota(jnp.int32, (size, size), 0)
    cols = lax.broadcasted_iota(jnp.int32, (size, size), 1)
    return (rows == cols).astype(F32).astype(BF16)


def one_hot(index, width, first=0):
    lanes = lax.broadcasted_iota(jnp.int32, (index.shape[0], width), 1)
    return (lanes == index - first).astype(F32).astype(BF16)


TILES = [(w * 256, min(256, D - w * 256)) for w in range(5)]


def split_kernel(k_ref, v_ref, q_ref, s_ref, out_ref):
    for i, ref in enumerate((k_ref, v_ref, q_ref, s_ref)):
        for start, size in TILES:
            turned = nt(eye(size), ref[:, start : start + size])
            for h in range(H):
                low, high = max(h * HD, start), min((h + 1) * HD, start + size)
                if low < high:
                    out_ref[h, i * HD + low - h * HD : i * HD + high - h * HD, :] = turned[
                        low - start : high - start
                    ].astype(BF16)


def prepare(r_ref, k_ref, v_ref):
    for j in range(16):
        k_ref[j * TL : (j + 1) * TL, :] = nt(eye(TL), r_ref[j, :HD, :]).astype(BF16)
        v_ref[:HD, j * TL : (j + 1) * TL] = r_ref[j, HD : 2 * HD, :]
        v_ref[HD:, j * TL : (j + 1) * TL] = jnp.ones((8, TL), BF16)


def score_part(q, k_ref, s_ref, j, top):
    scores = nn(k_ref[j * 512 : (j + 1) * 512, :], q)
    s_ref[j * 512 : (j + 1) * 512, :] = scores
    for b in range(64):
        part = scores[b * 8 : (b + 1) * 8]
        top = part if top is None else jnp.maximum(top, part)
    return top


def value_part(top, v_ref, s_ref, j, total):
    weights = jnp.exp((s_ref[j * TL : (j + 1) * TL, :] - top) * SCALE).astype(BF16)
    part = nn(v_ref[:, j * TL : (j + 1) * TL], weights)
    return part if total is None else total + part


def interleave(q, top, k_ref, v_ref, next_ref, s_ref):
    new_top, total = None, None
    for j in range(16):
        if q is not None and j % 2 == 0:
            new_top = score_part(q, k_ref, next_ref, j // 2, new_top)
        if top is not None:
            total = value_part(top, v_ref, s_ref, j, total)
    if q is not None:
        new_top = jnp.max(new_top, axis=0, keepdims=True)
    if top is not None:
        total = (total[:HD] / total[HD : HD + 1]).astype(BF16)
    return new_top, total


def picked_kernel(idx_ref, r_ref, out_ref, k_ref, v_ref, s_ref, rows_ref):
    prepare(r_ref, k_ref, v_ref)
    lines = lax.broadcasted_iota(jnp.int32, (TL, TL), 0)
    for i in range(3):
        index = idx_ref[:, i * TL : (i + 1) * TL]
        rows = None
        for j in range(16):
            table = (lines == index - j * TL).astype(F32).astype(BF16)
            part = nn(r_ref[j, 2 * HD :, :], table)
            rows = part if rows is None else rows + part
        rows_ref[i] = rows.astype(BF16)
    top = None
    for i in range(4):
        q = rows_ref[i, :HD, :] if i < 3 else None
        top, done = interleave(q, top, k_ref, v_ref, s_ref.at[i % 2], s_ref.at[1 - i % 2])
        if i > 0:
            both = jnp.concatenate([done, rows_ref[i - 1, HD:, :]], axis=0)
            out_ref[(i - 1) * TL : i * TL, :] = nt(eye(TL), both).astype(BF16)


def main_kernel(steps, aliased, *refs):
    first_ref, q_ref, k_ref, v_ref = refs[:4]
    out_ref, s_ref, top_ref = refs[4 + aliased :]
    step = pl.program_id(0)

    @pl.when(step == 0)
    def _():
        top, _ = interleave(first_ref[0], None, k_ref, v_ref, s_ref.at[0], None)
        top_ref[0] = jnp.broadcast_to(top, (8, TL))

    def one(now, last):
        q = None if last else q_ref[0]
        top, done = interleave(
            q, top_ref[now, 0:1, :], k_ref, v_ref, s_ref.at[1 - now], s_ref.at[now]
        )
        if not last:
            top_ref[1 - now] = jnp.broadcast_to(top, (8, TL))
        out_ref[0] = done

    for now in range(2):

        @pl.when((step < steps - 1) & (lax.rem(step, 2) == now))
        def _(now=now):
            one(now, False)

    @pl.when(step == steps - 1)
    def _():
        one((steps - 1) % 2, True)


def main_part(heads, keys, values, first, steps, before=None):
    aliased = int(before is not None)
    head_block = lambda f: pl.BlockSpec((1, HD, TL), f)
    whole = lambda shape: pl.BlockSpec(shape, lambda i: (0, 0))
    in_specs = [
        head_block(lambda i: (first, 2, 0)),
        head_block(lambda i: (first + jnp.minimum(i + 1, steps - 1), 2, 0)),
        whole((4096, HD)),
        whole((80, 4096)),
    ] + [pl.BlockSpec(memory_space=pl.ANY)] * aliased
    return pl.pallas_call(
        functools.partial(main_kernel, steps, aliased),
        grid=(steps,),
        in_specs=in_specs,
        out_specs=head_block(lambda i: (first + i, 1, 0)),
        out_shape=shaped(16, 2 * HD, TL),
        scratch_shapes=[pltpu.VMEM((2, 4096, TL), F32), pltpu.VMEM((2, 8, TL), F32)],
        input_output_aliases={4: 0} if aliased else {},
        compiler_params=pltpu.CompilerParams(vmem_limit_bytes=18 << 20),
        cost_estimate=pl.CostEstimate(
            flops=steps * 4 * 256 * 4096 * 256, transcendentals=steps * 256 * 4096, bytes_accessed=2 << 20
        ),
        name="main_attention",
    )(*in_hbm(heads, heads, keys, values, *([before] if aliased else [])))


def normed_kernel(x_ref, w_ref, b_ref, mod_ref, out_ref, att_ref, str_ref):
    for h in range(H):
        att_ref[:, h * HD : (h + 1) * HD] = x_ref[h, :, :HD].astype(F32)
        str_ref[:, h * HD : (h + 1) * HD] = x_ref[h, :, HD:].astype(F32)
    projected = nn(att_ref[...].astype(BF16), w_ref[...]) + b_ref[...]
    residual = (str_ref[...] + mod_ref[0:1, :] * projected).astype(BF16).astype(F32)
    centred = residual - jnp.mean(residual, axis=1, keepdims=True)
    variance = jnp.mean(centred * centred, axis=1, keepdims=True)
    normed = centred * lax.rsqrt(variance + 1e-06) * (1.0 + mod_ref[2:3, :]) + mod_ref[1:2, :]
    att_ref[...] = normed
    for e in range(16):
        out_ref[e] = att_ref[3 * e : 3 * e + 3, :].astype(BF16)


def compact_kernel(x_ref, idx_ref, out_ref, rows_ref):
    for g in range(16):
        rows_ref[3 * g : 3 * g + 3, :] = x_ref[g].astype(F32)
    lines = lax.broadcasted_iota(jnp.int32, (16, 48), 0)
    table = (lines == idx_ref[...]).astype(F32).astype(BF16)
    rows = nn(table, rows_ref[...].astype(BF16)).astype(BF16)
    for t in range(16):
        out_ref[t] = rows


def expert_kernel(x_ref, we_ref, be_ref, wr_ref, router_ref, _, out_ref, gate_ref):
    rows = x_ref[...]
    hidden = jax.nn.gelu(nn(rows, we_ref[...]) + be_ref[...], approximate=True).astype(BF16)
    for c in range(16):
        out_ref[c] = nt(wr_ref[c], hidden).astype(BF16)
    gate_ref[...] = jax.nn.sigmoid(nt(router_ref[...], rows)).astype(BF16).astype(F32)


def gather_kernel(x_ref, gate_ref, rb_ref, idx_ref, out_ref):
    total = x_ref[0, :HD, :].astype(F32)
    for t in range(1, 16):
        total = total + x_ref[t, :HD, :].astype(F32)
    rows = (total + rb_ref[...]).astype(BF16).astype(F32)
    rows = (rows * gate_ref[0:1, :]).astype(BF16)
    for i in range(3):
        index = idx_ref[i * 256 : (i + 1) * 256, :]
        out_ref[i * 256 : (i + 1) * 256, :] = nt(one_hot(index, 256), rows).astype(BF16)


def scatter_kernel(p_ref, idx_ref, out_ref):
    turned = nt(eye(HD), p_ref[...]).astype(BF16)
    index = idx_ref[...]
    for t in range(16):
        out_ref[t] = nn(turned, one_hot(index, TL, t * TL)).astype(BF16)


def residual_kernel(o_ref, s_ref, w_ref, b_ref, mod_ref, out_ref, att_ref):
    for h in range(H):
        att_ref[h * HD : (h + 1) * HD, :] = o_ref[h, HD:, :]
    projected = None
    for start, size in TILES:
        rows = nt(eye(TL), att_ref[start : start + size, :]).astype(BF16)
        part = nn(rows, w_ref[start : start + size, :])
        projected = part if projected is None else projected + part
    projected = projected + b_ref[...]
    out_ref[...] = (s_ref[...].astype(F32) + mod_ref[0:1, :] * projected).astype(BF16)


def final_kernel(m_ref, res_ref, mod_ref, out_ref, mix_ref):
    for c in range(16):
        mix_ref[c * HD : (c + 1) * HD, :] = m_ref[c]
    for start, size in TILES:
        cols = slice(start, start + size)
        mixed = nt(eye(TL), mix_ref[cols, :])
        out_ref[:, cols] = (
            res_ref[:, cols].astype(F32) + mod_ref[3:4, cols] * mixed
        ).astype(BF16)


def call(kernel, out_shape, name, mib, scratch=()):
    return pl.pallas_call(
        kernel,
        out_shape=out_shape,
        scratch_shapes=list(scratch),
        compiler_params=pltpu.CompilerParams(vmem_limit_bytes=mib << 20),
        name=name,
    )


def shaped(*shape, dtype=BF16):
    return pltpu.HBM(shape, dtype)


def in_hbm(*arrays):
    return [pltpu.with_memory_space_constraint(array, pltpu.HBM) for array in arrays]


def per_device(
    stream,
    queries,
    key_vectors,
    value_vectors,
    modulation,
    output_weight,
    output_bias,
    router_weight,
    expand_weight,
    expand_bias,
    reduce_weight,
    reduce_bias,
    counts,
    picked_rows,
):
    me_frame = lax.axis_index("frame").astype(jnp.int32)
    me_tok = lax.axis_index("tok").astype(jnp.int32)
    exchange = functools.partial(lax.all_to_all, split_axis=0, concat_axis=0, tiled=True)
    mod = modulation[0]
    out_bias = output_bias[None, :]

    sent = call(split_kernel, shaped(16, 4 * HD, TL), "split", 12)(
        *in_hbm(key_vectors[0], value_vectors[0], queries[0], stream[0])
    )
    heads = exchange(sent, "tok")

    own_counts = counts[:, 0]
    all_counts = lax.all_gather(own_counts, "frame", axis=1)
    frames = jnp.arange(16, dtype=jnp.int32)
    before = (frames[:, None] < frames[None, :]).astype(jnp.int32)
    offsets = jnp.sum(all_counts[:, :, None] * before[None, :, :], axis=1)
    is_own = (frames == me_frame).astype(jnp.int32)
    own_offsets = jnp.sum(offsets * is_own[None, :], axis=1)
    expert_offsets = jnp.sum(offsets * is_own[:, None], axis=0)
    expert_counts = jnp.sum(all_counts * is_own[:, None], axis=0)
    picked = picked_rows[:, 0, :]
    slots = jnp.arange(48, dtype=jnp.int32)
    thirds = jnp.arange(3, dtype=jnp.int32) * 16
    pick_slot = ((frames[:, None] - own_offsets[None, :]) & 15)[:, :, None] + thirds
    pick_pos = jnp.sum(
        jnp.where(pick_slot[:, :, :, None] == slots, picked[None, :, None, :], 0), axis=3
    )
    pick_index = jnp.where(pick_slot < own_counts[None, :, None], pick_pos, -1).reshape(1, 768)
    held_slot = ((me_tok - expert_offsets) & 15)[:, None] + thirds
    held_index = jnp.where(
        held_slot < expert_counts[:, None], (expert_offsets[:, None] + held_slot) >> 4, -1
    ).reshape(1, 48)
    row_id = expert_offsets[:, None] + slots[None, :]
    back_index = jnp.where(
        slots[None, :] < expert_counts[:, None], (row_id & 15) * 16 + (row_id >> 4), -1
    ).reshape(768, 1)
    spread_index = jnp.where(slots[None, :] < own_counts[:, None], picked, -1).reshape(768, 1)

    router_own = jnp.sum(
        jnp.where((frames == me_frame)[None, :], router_weight, jnp.zeros_like(router_weight)), axis=1
    )
    router_rows = jnp.broadcast_to(router_own[None, :], (8, D))
    bias_own = lax.dynamic_slice_in_dim(reduce_bias[0].reshape(16, HD), me_tok, 1, 0).reshape(HD, 1)
    reduce_turned = reduce_weight[0].T.reshape(16, HD, 288)

    picked_out, keys, values = call(
        picked_kernel,
        (shaped(768, 2 * HD), shaped(4096, HD), shaped(80, 4096)),
        "picked_attention",
        24,
        [pltpu.VMEM((2, 4096, TL), F32), pltpu.VMEM((3, 2 * HD, TL), BF16)],
    )(pick_index, heads)

    rows = exchange(picked_out.reshape(16, 48, 2 * HD), "tok")
    attended = main_part(heads, keys, values, 0, 5)
    rows, attended = lax.optimization_barrier((rows, attended))
    normed = call(
        normed_kernel, shaped(16, 3, D), "normed", 10, [pltpu.VMEM((48, D), F32), pltpu.VMEM((48, D), F32)]
    )(rows, output_weight, out_bias, mod)
    normed = exchange(normed, "frame")
    attended = main_part(heads, keys, values, 5, 6, attended)
    normed, attended = lax.optimization_barrier((normed, attended))
    rows = call(compact_kernel, shaped(16, 16, D), "compact", 6, [pltpu.VMEM((48, D), F32)])(
        normed, held_index
    )
    rows = exchange(rows, "tok")
    attended = main_part(heads, keys, values, 11, 5, attended)
    rows, attended = lax.optimization_barrier((rows, attended))
    whole = lambda shape: pl.BlockSpec(shape, lambda i: (0,) * len(shape))
    both, gates = pl.pallas_call(
        expert_kernel,
        grid=(1,),
        in_specs=[
            whole((TL, D)),
            whole((D, 288)),
            whole((1, 288)),
            whole((16, HD, 288)),
            whole((8, D)),
            pl.BlockSpec(memory_space=pl.ANY),
        ],
        out_specs=(whole((16, HD, TL)), whole((8, TL))),
        out_shape=(shaped(16, 2 * HD, TL), shaped(8, TL, dtype=F32)),
        input_output_aliases={5: 0},
        compiler_params=pltpu.CompilerParams(vmem_limit_bytes=12 << 20),
        name="expert",
    )(rows.reshape(TL, D), *in_hbm(expand_weight[0], expand_bias, reduce_turned, router_rows, attended))
    both = exchange(both, "tok")
    outs = call(gather_kernel, shaped(768, HD), "weighted", 8)(both, *in_hbm(gates, bias_own, back_index))
    outs = exchange(outs.reshape(16, 48, HD), "frame")
    residual = call(residual_kernel, shaped(TL, D), "residual", 12, [pltpu.VMEM((D, TL), BF16)])(
        *in_hbm(both, stream[0], output_weight, out_bias, mod)
    )
    mixed = call(scatter_kernel, shaped(16, HD, TL), "scatter", 8)(outs.reshape(768, HD), *in_hbm(spread_index))
    mixed = exchange(mixed, "tok")
    layer_out = call(final_kernel, shaped(TL, D), "final", 8, [pltpu.VMEM((D, TL), BF16)])(
        mixed, *in_hbm(residual, mod)
    )
    return layer_out[None]


def solution(mesh):
    return jax.shard_map(
        per_device,
        mesh=mesh,
        in_specs=(
            P("frame", "tok", None),
            P("frame", "tok", None),
            P("frame", "tok", None),
            P("frame", "tok", None),
            P("frame", None, None),
            P(),
            P(),
            P(),
            P("frame", None, "tok"),
            P("frame", "tok"),
            P("frame", "tok", None),
            P("frame", None),
            P(None, "frame"),
            P(None, "frame", None),
        ),
        out_specs=P("frame", "tok", None),
        check_vma=False,
    )
```

```python
import functools
import math

import jax
import jax.numpy as jnp
from jax import lax
from jax.experimental import pallas as pl
from jax.experimental.pallas import tpu as pltpu
from jax.sharding import PartitionSpec as P

H = 16
HD = 72
D = 1152
TL = 256
F32 = jnp.float32
BF16 = jnp.bfloat16
SCALE = 1.0 / math.sqrt(HD)


def nt(left, right):
    return lax.dot_general(left, right, (((1,), (1,)), ((), ())), preferred_element_type=F32)


def nn(left, right):
    return jnp.dot(left, right, preferred_element_type=F32)


def eye(size):
    rows = lax.broadcasted_iota(jnp.int32, (size, size), 0)
    cols = lax.broadcasted_iota(jnp.int32, (size, size), 1)
    return (rows == cols).astype(F32).astype(BF16)


def one_hot(index, width, first=0):
    lanes = lax.broadcasted_iota(jnp.int32, (index.shape[0], width), 1)
    return (lanes == index - first).astype(F32).astype(BF16)


TILES = [(w * 256, min(256, D - w * 256)) for w in range(5)]


def copy(source, target, sem):
    return pltpu.make_async_copy(source, target, sem)


def split_kernel(k_ref, v_ref, q_ref, s_ref, out_ref, in_ref, turned_ref, in_sem, out_sem):
    loads = [copy(ref, in_ref.at[i], in_sem.at[i]) for i, ref in enumerate((k_ref, v_ref, q_ref, s_ref))]
    for load in loads:
        load.start()
    stores = []
    for i, load in enumerate(loads):
        load.wait()
        for start, size in TILES:
            turned = nt(eye(size), in_ref[i, :, start : start + size])
            for h in range(H):
                low, high = max(h * HD, start), min((h + 1) * HD, start + size)
                if low < high:
                    turned_ref[i, h, low - h * HD : high - h * HD, :] = turned[
                        low - start : high - start
                    ].astype(BF16)
        stores.append(
            copy(turned_ref.at[i], out_ref.at[:, i * HD : (i + 1) * HD, :], out_sem.at[i])
        )
        stores[-1].start()
    for store in stores:
        store.wait()


def prepare(r_ref, k_ref, v_ref):
    for j in range(16):
        k_ref[j * TL : (j + 1) * TL, :] = nt(eye(TL), r_ref[j, :HD, :]).astype(BF16)
        v_ref[:HD, j * TL : (j + 1) * TL] = r_ref[j, HD : 2 * HD, :]
        v_ref[HD:, j * TL : (j + 1) * TL] = jnp.ones((8, TL), BF16)


def score_part(q, k_ref, s_ref, j, top):
    scores = nn(k_ref[j * 512 : (j + 1) * 512, :], q)
    s_ref[j * 512 : (j + 1) * 512, :] = scores
    for b in range(64):
        part = scores[b * 8 : (b + 1) * 8]
        top = part if top is None else jnp.maximum(top, part)
    return top


def value_part(top, v_ref, s_ref, j, total):
    weights = jnp.exp((s_ref[j * TL : (j + 1) * TL, :] - top) * SCALE).astype(BF16)
    part = nn(v_ref[:, j * TL : (j + 1) * TL], weights)
    return part if total is None else total + part


def interleave(q, top, k_ref, v_ref, next_ref, s_ref):
    new_top, total = None, None
    for j in range(16):
        if q is not None and j % 2 == 0:
            new_top = score_part(q, k_ref, next_ref, j // 2, new_top)
        if top is not None:
            total = value_part(top, v_ref, s_ref, j, total)
    if q is not None:
        new_top = jnp.max(new_top, axis=0, keepdims=True)
    if top is not None:
        total = (total[:HD] / total[HD : HD + 1]).astype(BF16)
    return new_top, total


def picked_kernel(
    idx_ref, r_ref, out_ref, keys_ref, values_ref, k_ref, v_ref, s_ref, rows_ref, done_ref, sem
):
    prepare(r_ref, k_ref, v_ref)
    stores = [copy(k_ref, keys_ref, sem.at[0]), copy(v_ref, values_ref, sem.at[1])]
    for store in stores:
        store.start()
    lines = lax.broadcasted_iota(jnp.int32, (TL, TL), 0)
    for i in range(3):
        index = idx_ref[:, i * TL : (i + 1) * TL]
        rows = None
        for j in range(16):
            table = (lines == index - j * TL).astype(F32).astype(BF16)
            part = nn(r_ref[j, 2 * HD :, :], table)
            rows = part if rows is None else rows + part
        rows_ref[i] = rows.astype(BF16)
    top = None
    for i in range(4):
        q = rows_ref[i, :HD, :] if i < 3 else None
        top, done = interleave(q, top, k_ref, v_ref, s_ref.at[i % 2], s_ref.at[1 - i % 2])
        if i > 0:
            both = jnp.concatenate([done, rows_ref[i - 1, HD:, :]], axis=0)
            block = slice((i - 1) * TL, i * TL)
            done_ref[block, :] = nt(eye(TL), both).astype(BF16)
            stores.append(copy(done_ref.at[block, :], out_ref.at[block, :], sem.at[i + 1]))
            stores[-1].start()
    for store in stores:
        store.wait()


def main_kernel(steps, aliased, *refs):
    first_ref, q_ref, keys_ref, values_ref = refs[:4]
    out_ref, s_ref, top_ref, k_ref, v_ref, sem = refs[4 + aliased :]
    step = pl.program_id(0)

    @pl.when(step == 0)
    def _():
        loads = [
            copy(keys_ref.at[j * 512 : (j + 1) * 512, :], k_ref.at[j * 512 : (j + 1) * 512, :], sem.at[j])
            for j in range(8)
        ] + [copy(values_ref, v_ref, sem.at[8])]
        for load in loads:
            load.start()
        top = None
        for j in range(8):
            loads[j].wait()
            top = score_part(first_ref[0], k_ref, s_ref.at[0], j, top)
        top = jnp.max(top, axis=0, keepdims=True)
        loads[8].wait()
        top_ref[0] = jnp.broadcast_to(top, (8, TL))

    def one(now, last):
        q = None if last else q_ref[0]
        top, done = interleave(
            q, top_ref[now, 0:1, :], k_ref, v_ref, s_ref.at[1 - now], s_ref.at[now]
        )
        if not last:
            top_ref[1 - now] = jnp.broadcast_to(top, (8, TL))
        out_ref[0] = done

    for now in range(2):

        @pl.when((step < steps - 1) & (lax.rem(step, 2) == now))
        def _(now=now):
            one(now, False)

    @pl.when(step == steps - 1)
    def _():
        one((steps - 1) % 2, True)


def main_part(heads, keys, values, first, steps, before=None):
    aliased = int(before is not None)
    head_block = lambda f: pl.BlockSpec((1, HD, TL), f)
    in_specs = [
        head_block(lambda i: (first, 2, 0)),
        head_block(lambda i: (first + jnp.minimum(i + 1, steps - 1), 2, 0)),
    ] + [pl.BlockSpec(memory_space=pl.ANY)] * (2 + aliased)
    return pl.pallas_call(
        functools.partial(main_kernel, steps, aliased),
        grid=(steps,),
        in_specs=in_specs,
        out_specs=head_block(lambda i: (first + i, 1, 0)),
        out_shape=shaped(16, 2 * HD, TL),
        scratch_shapes=[
            pltpu.VMEM((2, 4096, TL), F32),
            pltpu.VMEM((2, 8, TL), F32),
            pltpu.VMEM((4096, HD), BF16),
            pltpu.VMEM((80, 4096), BF16),
            pltpu.SemaphoreType.DMA((9,)),
        ],
        input_output_aliases={4: 0} if aliased else {},
        compiler_params=pltpu.CompilerParams(vmem_limit_bytes=18 << 20),
        cost_estimate=pl.CostEstimate(
            flops=steps * 4 * 256 * 4096 * 256, transcendentals=steps * 256 * 4096, bytes_accessed=2 << 20
        ),
        name="main_attention",
    )(*in_hbm(heads, heads, keys, values, *([before] if aliased else [])))


def normed_kernel(x_ref, w_ref, b_ref, mod_ref, out_ref, att_ref, str_ref):
    for h in range(H):
        att_ref[:, h * HD : (h + 1) * HD] = x_ref[h, :, :HD].astype(F32)
        str_ref[:, h * HD : (h + 1) * HD] = x_ref[h, :, HD:].astype(F32)
    projected = nn(att_ref[...].astype(BF16), w_ref[...]) + b_ref[...]
    residual = (str_ref[...] + mod_ref[0:1, :] * projected).astype(BF16).astype(F32)
    centred = residual - jnp.mean(residual, axis=1, keepdims=True)
    variance = jnp.mean(centred * centred, axis=1, keepdims=True)
    normed = centred * lax.rsqrt(variance + 1e-06) * (1.0 + mod_ref[2:3, :]) + mod_ref[1:2, :]
    att_ref[...] = normed
    for e in range(16):
        out_ref[e] = att_ref[3 * e : 3 * e + 3, :].astype(BF16)


def compact_kernel(x_ref, idx_ref, out_ref, rows_ref):
    for g in range(16):
        rows_ref[3 * g : 3 * g + 3, :] = x_ref[g].astype(F32)
    lines = lax.broadcasted_iota(jnp.int32, (16, 48), 0)
    table = (lines == idx_ref[...]).astype(F32).astype(BF16)
    rows = nn(table, rows_ref[...].astype(BF16)).astype(BF16)
    for t in range(16):
        out_ref[t] = rows


def expert_kernel(
    x_ref, be_ref, router_ref, we_ref, wr_ref, _, out_ref, gate_ref, we_s, wr_s, part_ref, sem
):
    loads = [copy(we_ref, we_s, sem.at[0]), copy(wr_ref, wr_s, sem.at[1])]
    for load in loads:
        load.start()
    rows = x_ref[...]
    router = jnp.broadcast_to(router_ref[...].astype(F32), (8, D)).astype(BF16)
    gate_ref[...] = jax.nn.sigmoid(nt(router, rows)).astype(BF16).astype(F32)
    loads[0].wait()
    hidden = jax.nn.gelu(nt(rows, we_s[...]) + be_ref[...], approximate=True).astype(BF16)
    loads[1].wait()
    stores = []
    for c in range(16):
        part_ref[c] = nt(wr_s[c], hidden).astype(BF16)
        if c % 4 == 3:
            block = slice(c - 3, c + 1)
            stores.append(copy(part_ref.at[block], out_ref.at[block, :HD, :], sem.at[2 + c // 4]))
            stores[-1].start()
    for store in stores:
        store.wait()


def weighted_kernel(x_ref, gate_ref, rb_ref, idx_ref, out_ref):
    total = x_ref[0].astype(F32)
    for t in range(1, 16):
        total = total + x_ref[t].astype(F32)
    rows = (total + rb_ref[...]).astype(BF16).astype(F32)
    rows = (rows * gate_ref[0:1, :]).astype(BF16)
    lines = lax.broadcasted_iota(jnp.int32, (TL, TL), 0)
    for i in range(3):
        block = slice(i * TL, (i + 1) * TL)
        table = (lines == idx_ref[:, block]).astype(F32).astype(BF16)
        out_ref[block, :] = nt(eye(TL), nn(rows, table).astype(BF16)).astype(BF16)


def scatter_kernel(p_ref, idx_ref, out_ref, mix_ref, sem):
    turned = nt(eye(HD), p_ref[...]).astype(BF16)
    index = idx_ref[...]
    lines = lax.broadcasted_iota(jnp.int32, (TL, 768), 0)
    stores = []
    for t in range(16):
        table = (lines == index - t * TL).astype(F32).astype(BF16)
        mix_ref[t] = nt(turned, table).astype(BF16)
        if t % 4 == 3:
            block = slice(t - 3, t + 1)
            stores.append(copy(mix_ref.at[block], out_ref.at[block], sem.at[t // 4]))
            stores[-1].start()
    for store in stores:
        store.wait()


def residual_kernel(o_ref, s_ref, w_ref, b_ref, mod_ref, out_ref, att_ref):
    for h in range(H):
        att_ref[h * HD : (h + 1) * HD, :] = o_ref[h, HD:, :]
    projected = None
    for start, size in TILES:
        rows = nt(eye(TL), att_ref[start : start + size, :]).astype(BF16)
        part = nn(rows, w_ref[start : start + size, :])
        projected = part if projected is None else projected + part
    projected = projected + b_ref[...]
    out_ref[...] = (s_ref[...].astype(F32) + mod_ref[0:1, :] * projected).astype(BF16)


def final_kernel(m_ref, res_ref, mod_ref, out_ref):
    mixed = nt(eye(TL), m_ref[...])
    out_ref[...] = (res_ref[...].astype(F32) + mod_ref[3:4, :] * mixed).astype(BF16)


ANY = pl.BlockSpec(memory_space=pl.ANY)
VMEM = pl.BlockSpec(memory_space=pltpu.VMEM)


def call(kernel, out_shape, name, mib, scratch=(), **specs):
    return pl.pallas_call(
        kernel,
        out_shape=out_shape,
        **specs,
        scratch_shapes=list(scratch),
        compiler_params=pltpu.CompilerParams(vmem_limit_bytes=mib << 20),
        name=name,
    )


def shaped(*shape, dtype=BF16):
    return pltpu.HBM(shape, dtype)


def in_hbm(*arrays):
    return [pltpu.with_memory_space_constraint(array, pltpu.HBM) for array in arrays]


def per_device(
    stream,
    queries,
    key_vectors,
    value_vectors,
    modulation,
    output_weight,
    output_bias,
    router_weight,
    expand_weight,
    expand_bias,
    reduce_weight,
    reduce_bias,
    counts,
    picked_rows,
):
    me_frame = lax.axis_index("frame").astype(jnp.int32)
    me_tok = lax.axis_index("tok").astype(jnp.int32)
    exchange = functools.partial(lax.all_to_all, split_axis=0, concat_axis=0, tiled=True)
    mod = modulation[0]
    out_bias = output_bias[None, :]

    sent = call(
        split_kernel,
        shaped(16, 4 * HD, TL),
        "split",
        12,
        [
            pltpu.VMEM((4, TL, D), BF16),
            pltpu.VMEM((4, 16, HD, TL), BF16),
            pltpu.SemaphoreType.DMA((4,)),
            pltpu.SemaphoreType.DMA((4,)),
        ],
        in_specs=[ANY] * 4,
        out_specs=ANY,
    )(
        *in_hbm(key_vectors[0], value_vectors[0], queries[0], stream[0])
    )
    heads = exchange(sent, "tok")

    own_counts = counts[:, 0]
    all_counts = lax.all_gather(own_counts, "frame", axis=1)
    frames = jnp.arange(16, dtype=jnp.int32)
    before = (frames[:, None] < frames[None, :]).astype(jnp.int32)
    offsets = jnp.sum(all_counts[:, :, None] * before[None, :, :], axis=1)
    is_own = (frames == me_frame).astype(jnp.int32)
    own_offsets = jnp.sum(offsets * is_own[None, :], axis=1)
    expert_offsets = jnp.sum(offsets * is_own[:, None], axis=0)
    expert_counts = jnp.sum(all_counts * is_own[:, None], axis=0)
    picked = picked_rows[:, 0, :]
    slots = jnp.arange(48, dtype=jnp.int32)
    thirds = jnp.arange(3, dtype=jnp.int32) * 16
    pick_slot = ((frames[:, None] - own_offsets[None, :]) & 15)[:, :, None] + thirds
    pick_pos = jnp.sum(
        jnp.where(pick_slot[:, :, :, None] == slots, picked[None, :, None, :], 0), axis=3
    )
    pick_index = jnp.where(pick_slot < own_counts[None, :, None], pick_pos, -1).reshape(1, 768)
    held_slot = ((me_tok - expert_offsets) & 15)[:, None] + thirds
    held_index = jnp.where(
        held_slot < expert_counts[:, None], (expert_offsets[:, None] + held_slot) >> 4, -1
    ).reshape(1, 48)
    row_id = expert_offsets[:, None] + slots[None, :]
    back_index = jnp.where(
        slots[None, :] < expert_counts[:, None], (row_id & 15) * 16 + (row_id >> 4), -1
    ).reshape(1, 768)
    spread_index = jnp.where(slots[None, :] < own_counts[:, None], picked, -1).reshape(1, 768)

    router_own = jnp.sum(
        jnp.where((frames == me_frame)[None, :], router_weight, jnp.zeros_like(router_weight)), axis=1
    )
    router_own = router_own[None, :]
    bias_own = lax.dynamic_slice_in_dim(reduce_bias[0].reshape(16, HD), me_tok, 1, 0).reshape(HD, 1)
    reduce_turned = reduce_weight[0].T.reshape(16, HD, 288)
    expand_turned = expand_weight[0].T
    heads, reduce_turned, bias_own, back_index, spread_index, router_own = lax.optimization_barrier(
        (heads, reduce_turned, bias_own, back_index, spread_index, router_own)
    )

    picked_out, keys, values = call(
        picked_kernel,
        (shaped(768, 2 * HD), shaped(4096, HD), shaped(80, 4096)),
        "picked_attention",
        24,
        [
            pltpu.VMEM((4096, HD), BF16),
            pltpu.VMEM((80, 4096), BF16),
            pltpu.VMEM((2, 4096, TL), F32),
            pltpu.VMEM((3, 2 * HD, TL), BF16),
            pltpu.VMEM((768, 2 * HD), BF16),
            pltpu.SemaphoreType.DMA((5,)),
        ],
        in_specs=[VMEM, VMEM],
        out_specs=(ANY, ANY, ANY),
    )(pick_index, heads)

    rows = exchange(picked_out.reshape(16, 48, 2 * HD), "tok")
    attended = main_part(heads, keys, values, 0, 5)
    rows, attended = lax.optimization_barrier((rows, attended))
    normed = call(
        normed_kernel, shaped(16, 3, D), "normed", 10, [pltpu.VMEM((48, D), F32), pltpu.VMEM((48, D), F32)]
    )(rows, output_weight, out_bias, mod)
    normed = exchange(normed, "frame")
    attended = main_part(heads, keys, values, 5, 6, attended)
    normed, attended = lax.optimization_barrier((normed, attended))
    rows = call(compact_kernel, shaped(16, 16, D), "compact", 6, [pltpu.VMEM((48, D), F32)])(
        normed, held_index
    )
    rows = exchange(rows, "tok")
    attended = main_part(heads, keys, values, 11, 5, attended)
    rows, attended = lax.optimization_barrier((rows, attended))
    both, gates = call(
        expert_kernel,
        (shaped(16, 2 * HD, TL), shaped(8, TL, dtype=F32)),
        "expert",
        10,
        [
            pltpu.VMEM((288, D), BF16),
            pltpu.VMEM((16, HD, 288), BF16),
            pltpu.VMEM((16, HD, TL), BF16),
            pltpu.SemaphoreType.DMA((6,)),
        ],
        in_specs=[VMEM, VMEM, VMEM, ANY, ANY, ANY],
        out_specs=(ANY, VMEM),
        input_output_aliases={5: 0},
    )(
        rows.reshape(TL, D),
        *in_hbm(expand_bias, router_own, expand_turned, reduce_turned, attended),
    )
    both = exchange(both, "tok")
    first_block = lambda *shape: pl.BlockSpec(shape, lambda i: (0,) * len(shape))
    outs = call(
        weighted_kernel,
        shaped(768, HD),
        "weighted",
        8,
        grid=(1,),
        in_specs=[
            first_block(16, HD, TL),
            first_block(8, TL),
            first_block(HD, 1),
            first_block(1, 768),
        ],
        out_specs=first_block(768, HD),
    )(both, *in_hbm(gates, bias_own, back_index))
    outs = exchange(outs.reshape(16, 48, HD), "frame")
    residual = call(residual_kernel, shaped(TL, D), "residual", 12, [pltpu.VMEM((D, TL), BF16)])(
        *in_hbm(both, stream[0], output_weight, out_bias, mod)
    )
    mixed = call(
        scatter_kernel,
        shaped(16, HD, TL),
        "scatter",
        8,
        [pltpu.VMEM((16, HD, TL), BF16), pltpu.SemaphoreType.DMA((4,))],
        in_specs=[VMEM, VMEM],
        out_specs=ANY,
    )(outs.reshape(768, HD), *in_hbm(spread_index))
    mixed = exchange(mixed, "tok")
    layer_out = call(
        final_kernel,
        shaped(TL, D),
        "final",
        8,
        grid=(3,),
        in_specs=[
            pl.BlockSpec((384, TL), lambda i: (i, 0)),
            pl.BlockSpec((TL, 384), lambda i: (0, i)),
            pl.BlockSpec((4, 384), lambda i: (0, i)),
        ],
        out_specs=pl.BlockSpec((TL, 384), lambda i: (0, i)),
    )(mixed.reshape(D, TL), *in_hbm(residual, mod))
    return layer_out[None]


def solution(mesh):
    return jax.shard_map(
        per_device,
        mesh=mesh,
        in_specs=(
            P("frame", "tok", None),
            P("frame", "tok", None),
            P("frame", "tok", None),
            P("frame", "tok", None),
            P("frame", None, None),
            P(),
            P(),
            P(),
            P("frame", None, "tok"),
            P("frame", "tok"),
            P("frame", "tok", None),
            P("frame", None),
            P(None, "frame"),
            P(None, "frame", None),
        ),
        out_specs=P("frame", "tok", None),
        check_vma=False,
    )
```

```python
import functools
import math

import jax
import jax.numpy as jnp
from jax import lax
from jax.experimental import pallas as pl
from jax.experimental.pallas import tpu as pltpu
from jax.sharding import PartitionSpec as P

H = 16
HD = 72
D = 1152
TL = 256
F32 = jnp.float32
BF16 = jnp.bfloat16
SCALE = 1.0 / math.sqrt(HD)


def nt(left, right):
    return lax.dot_general(left, right, (((1,), (1,)), ((), ())), preferred_element_type=F32)


def nn(left, right):
    return jnp.dot(left, right, preferred_element_type=F32)


def eye(size):
    rows = lax.broadcasted_iota(jnp.int32, (size, size), 0)
    cols = lax.broadcasted_iota(jnp.int32, (size, size), 1)
    return (rows == cols).astype(F32).astype(BF16)


def one_hot(index, width, first=0):
    lanes = lax.broadcasted_iota(jnp.int32, (index.shape[0], width), 1)
    return (lanes == index - first).astype(F32).astype(BF16)


TILES = [(w * 256, min(256, D - w * 256)) for w in range(5)]


def copy(source, target, sem):
    return pltpu.make_async_copy(source, target, sem)


def split_kernel(k_ref, v_ref, q_ref, s_ref, out_ref, in_ref, turned_ref, in_sem, out_sem):
    loads = [copy(ref, in_ref.at[i], in_sem.at[i]) for i, ref in enumerate((k_ref, v_ref, q_ref, s_ref))]
    for load in loads:
        load.start()
    stores = []
    for i, load in enumerate(loads):
        load.wait()
        for start, size in TILES:
            turned = nt(eye(size), in_ref[i, :, start : start + size])
            for h in range(H):
                low, high = max(h * HD, start), min((h + 1) * HD, start + size)
                if low < high:
                    turned_ref[i, h, low - h * HD : high - h * HD, :] = turned[
                        low - start : high - start
                    ].astype(BF16)
        stores.append(
            copy(turned_ref.at[i], out_ref.at[:, i * HD : (i + 1) * HD, :], out_sem.at[i])
        )
        stores[-1].start()
    for store in stores:
        store.wait()


def prepare(r_ref, k_ref, v_ref):
    for j in range(16):
        keys = nt(eye(TL), r_ref[j, :HD, :])
        k_ref[j * TL : (j + 1) * TL, :] = jnp.concatenate(
            [keys, jnp.zeros((TL, 128 - HD), F32)], axis=1
        ).astype(BF16)
        v_ref[:HD, j * TL : (j + 1) * TL] = r_ref[j, HD : 2 * HD, :]
        v_ref[HD:, j * TL : (j + 1) * TL] = jnp.ones((8, TL), BF16)


def score_part(q, k_ref, s_ref, j, top):
    scores = nn(k_ref[j * 512 : (j + 1) * 512, :], q)
    s_ref[j * 512 : (j + 1) * 512, :] = scores
    for b in range(64):
        part = scores[b * 8 : (b + 1) * 8]
        top = part if top is None else jnp.maximum(top, part)
    return top


def value_part(top, v_ref, s_ref, j, total):
    weights = jnp.exp((s_ref[j * TL : (j + 1) * TL, :] - top) * SCALE).astype(BF16)
    part = nn(v_ref[:, j * TL : (j + 1) * TL], weights)
    return part if total is None else total + part


def padded(q):
    return jnp.concatenate([q.astype(F32), jnp.zeros((128 - HD, TL), F32)], axis=0).astype(BF16)


def interleave(q, top, k_ref, v_ref, next_ref, s_ref):
    new_top, total = None, None
    for j in range(16):
        if q is not None and j % 2 == 0:
            new_top = score_part(q, k_ref, next_ref, j // 2, new_top)
        if top is not None:
            total = value_part(top, v_ref, s_ref, j, total)
    if q is not None:
        new_top = jnp.max(new_top, axis=0, keepdims=True)
    if top is not None:
        total = (total[:HD] / total[HD : HD + 1]).astype(BF16)
    return new_top, total


def picked_kernel(
    idx_ref, r_ref, out_ref, keys_ref, values_ref, k_ref, v_ref, s_ref, rows_ref, done_ref, sem
):
    prepare(r_ref, k_ref, v_ref)
    stores = [copy(k_ref, keys_ref, sem.at[0]), copy(v_ref, values_ref, sem.at[1])]
    for store in stores:
        store.start()
    lines = lax.broadcasted_iota(jnp.int32, (TL, TL), 0)
    for i in range(3):
        index = idx_ref[:, i * TL : (i + 1) * TL]
        rows = None
        for j in range(16):
            table = (lines == index - j * TL).astype(F32).astype(BF16)
            part = nn(r_ref[j, 2 * HD :, :], table)
            rows = part if rows is None else rows + part
        rows_ref[i] = rows.astype(BF16)
    top = None
    for i in range(4):
        q = padded(rows_ref[i, :HD, :]) if i < 3 else None
        top, done = interleave(q, top, k_ref, v_ref, s_ref.at[i % 2], s_ref.at[1 - i % 2])
        if i > 0:
            both = jnp.concatenate([done, rows_ref[i - 1, HD:, :]], axis=0)
            block = slice((i - 1) * TL, i * TL)
            done_ref[block, :] = nt(eye(TL), both).astype(BF16)
            stores.append(copy(done_ref.at[block, :], out_ref.at[block, :], sem.at[i + 1]))
            stores[-1].start()
    for store in stores:
        store.wait()


def main_kernel(steps, aliased, *refs):
    first_ref, q_ref, k_ref, v_ref = refs[:4]
    out_ref, s_ref, top_ref = refs[4 + aliased :]
    step = pl.program_id(0)

    @pl.when(step == 0)
    def _():
        top, _ = interleave(padded(first_ref[0]), None, k_ref, v_ref, s_ref.at[0], None)
        top_ref[0] = jnp.broadcast_to(top, (8, TL))

    def one(now, last):
        q = None if last else padded(q_ref[0])
        top, done = interleave(
            q, top_ref[now, 0:1, :], k_ref, v_ref, s_ref.at[1 - now], s_ref.at[now]
        )
        if not last:
            top_ref[1 - now] = jnp.broadcast_to(top, (8, TL))
        out_ref[0] = done

    for now in range(2):

        @pl.when((step < steps - 1) & (lax.rem(step, 2) == now))
        def _(now=now):
            one(now, False)

    @pl.when(step == steps - 1)
    def _():
        one((steps - 1) % 2, True)


def main_part(heads, keys, values, first, steps, before=None):
    aliased = int(before is not None)
    head_block = lambda f: pl.BlockSpec((1, HD, TL), f)
    in_specs = [
        head_block(lambda i: (first, 2, 0)),
        head_block(lambda i: (first + jnp.minimum(i + 1, steps - 1), 2, 0)),
        pl.BlockSpec((4096, 128), lambda i: (0, 0)),
        pl.BlockSpec((80, 4096), lambda i: (0, 0)),
    ] + [pl.BlockSpec(memory_space=pl.ANY)] * aliased
    return pl.pallas_call(
        functools.partial(main_kernel, steps, aliased),
        grid=(steps,),
        in_specs=in_specs,
        out_specs=head_block(lambda i: (first + i, 1, 0)),
        out_shape=shaped(16, 2 * HD, TL),
        scratch_shapes=[
            pltpu.VMEM((2, 4096, TL), F32),
            pltpu.VMEM((2, 8, TL), F32),
        ],
        input_output_aliases={4: 0} if aliased else {},
        compiler_params=pltpu.CompilerParams(vmem_limit_bytes=18 << 20),
        cost_estimate=pl.CostEstimate(
            flops=steps * 4 * 256 * 4096 * 256, transcendentals=steps * 256 * 4096, bytes_accessed=2 << 20
        ),
        name="main_attention",
    )(*in_hbm(heads, heads, keys, values, *([before] if aliased else [])))


def normed_kernel(x_ref, w_ref, b_ref, mod_ref, out_ref, att_ref, str_ref):
    for h in range(H):
        att_ref[:, h * HD : (h + 1) * HD] = x_ref[h, :, :HD].astype(F32)
        str_ref[:, h * HD : (h + 1) * HD] = x_ref[h, :, HD : 2 * HD].astype(F32)
    projected = nn(att_ref[...].astype(BF16), w_ref[...]) + b_ref[...]
    residual = (str_ref[...] + mod_ref[0:1, :] * projected).astype(BF16).astype(F32)
    centred = residual - jnp.mean(residual, axis=1, keepdims=True)
    variance = jnp.mean(centred * centred, axis=1, keepdims=True)
    normed = centred * lax.rsqrt(variance + 1e-06) * (1.0 + mod_ref[2:3, :]) + mod_ref[1:2, :]
    att_ref[...] = normed
    for e in range(16):
        out_ref[e] = att_ref[3 * e : 3 * e + 3, :].astype(BF16)


def compact_kernel(x_ref, idx_ref, out_ref, rows_ref):
    for g in range(16):
        rows_ref[3 * g : 3 * g + 3, :] = x_ref[g].astype(F32)
    lines = lax.broadcasted_iota(jnp.int32, (16, 48), 0)
    table = (lines == idx_ref[...]).astype(F32).astype(BF16)
    rows = nn(table, rows_ref[...].astype(BF16)).astype(BF16)
    for t in range(16):
        out_ref[t] = rows


def expert_kernel(x_ref, be_ref, router_ref, we_ref, wr_ref, _, out_ref, gate_ref, part_ref, sem):
    rows = x_ref[...]
    router = jnp.broadcast_to(router_ref[...].astype(F32), (8, D)).astype(BF16)
    gate_ref[...] = jax.nn.sigmoid(nt(router, rows)).astype(BF16).astype(F32)
    hidden = jax.nn.gelu(nt(rows, we_ref[...]) + be_ref[...], approximate=True).astype(BF16)
    stores = []
    for c in range(16):
        part_ref[c] = nt(wr_ref[c], hidden).astype(BF16)
        if c % 4 == 3:
            block = slice(c - 3, c + 1)
            stores.append(copy(part_ref.at[block], out_ref.at[block, :HD, :], sem.at[c // 4]))
            stores[-1].start()
    for store in stores:
        store.wait()


def weighted_kernel(x_ref, gate_ref, rb_ref, idx_ref, out_ref):
    total = x_ref[0].astype(F32)
    for t in range(1, 16):
        total = total + x_ref[t].astype(F32)
    rows = (total + rb_ref[...]).astype(BF16).astype(F32)
    rows = (rows * gate_ref[0:1, :]).astype(BF16)
    lines = lax.broadcasted_iota(jnp.int32, (TL, TL), 0)
    for i in range(3):
        block = slice(i * TL, (i + 1) * TL)
        table = (lines == idx_ref[:, block]).astype(F32).astype(BF16)
        slots = jnp.concatenate([nn(rows, table), jnp.zeros((128 - HD, TL), F32)], axis=0)
        out_ref[block, :] = nt(eye(TL), slots.astype(BF16)).astype(BF16)


def scatter_kernel(p_ref, idx_ref, out_ref, mix_ref, sem):
    turned = nt(eye(128)[:HD], p_ref[...]).astype(BF16)
    index = idx_ref[...]
    lines = lax.broadcasted_iota(jnp.int32, (TL, 768), 0)
    stores = []
    for t in range(16):
        table = (lines == index - t * TL).astype(F32).astype(BF16)
        mix_ref[t] = nt(turned, table).astype(BF16)
        if t % 4 == 3:
            block = slice(t - 3, t + 1)
            stores.append(copy(mix_ref.at[block], out_ref.at[block], sem.at[t // 4]))
            stores[-1].start()
    for store in stores:
        store.wait()


def residual_kernel(o_ref, s_ref, w_ref, b_ref, mod_ref, out_ref, att_ref):
    for h in range(H):
        att_ref[h * HD : (h + 1) * HD, :] = o_ref[h, HD:, :]
    projected = None
    for start, size in TILES:
        rows = nt(eye(TL), att_ref[start : start + size, :]).astype(BF16)
        part = nn(rows, w_ref[start : start + size, :])
        projected = part if projected is None else projected + part
    projected = projected + b_ref[...]
    out_ref[...] = (s_ref[...].astype(F32) + mod_ref[0:1, :] * projected).astype(BF16)


def final_kernel(m_ref, res_ref, mod_ref, out_ref):
    for start, size in TILES:
        cols = slice(start, start + size)
        mixed = nt(eye(TL), m_ref[cols, :])
        out_ref[:, cols] = (res_ref[:, cols].astype(F32) + mod_ref[3:4, cols] * mixed).astype(BF16)


ANY = pl.BlockSpec(memory_space=pl.ANY)
VMEM = pl.BlockSpec(memory_space=pltpu.VMEM)


def call(kernel, out_shape, name, mib, scratch=(), **specs):
    return pl.pallas_call(
        kernel,
        out_shape=out_shape,
        **specs,
        scratch_shapes=list(scratch),
        compiler_params=pltpu.CompilerParams(vmem_limit_bytes=mib << 20),
        name=name,
    )


def shaped(*shape, dtype=BF16):
    return pltpu.HBM(shape, dtype)


def in_hbm(*arrays):
    return [pltpu.with_memory_space_constraint(array, pltpu.HBM) for array in arrays]


def per_device(
    stream,
    queries,
    key_vectors,
    value_vectors,
    modulation,
    output_weight,
    output_bias,
    router_weight,
    expand_weight,
    expand_bias,
    reduce_weight,
    reduce_bias,
    counts,
    picked_rows,
):
    me_frame = lax.axis_index("frame").astype(jnp.int32)
    me_tok = lax.axis_index("tok").astype(jnp.int32)
    exchange = functools.partial(lax.all_to_all, split_axis=0, concat_axis=0, tiled=True)
    mod = modulation[0]
    out_bias = output_bias[None, :]

    sent = call(
        split_kernel,
        shaped(16, 4 * HD, TL),
        "split",
        12,
        [
            pltpu.VMEM((4, TL, D), BF16),
            pltpu.VMEM((4, 16, HD, TL), BF16),
            pltpu.SemaphoreType.DMA((4,)),
            pltpu.SemaphoreType.DMA((4,)),
        ],
        in_specs=[ANY] * 4,
        out_specs=ANY,
    )(
        *in_hbm(key_vectors[0], value_vectors[0], queries[0], stream[0])
    )
    heads = exchange(sent, "tok")

    own_counts = counts[:, 0]
    all_counts = lax.all_gather(own_counts, "frame", axis=1)
    frames = jnp.arange(16, dtype=jnp.int32)
    before = (frames[:, None] < frames[None, :]).astype(jnp.int32)
    offsets = jnp.sum(all_counts[:, :, None] * before[None, :, :], axis=1)
    is_own = (frames == me_frame).astype(jnp.int32)
    own_offsets = jnp.sum(offsets * is_own[None, :], axis=1)
    expert_offsets = jnp.sum(offsets * is_own[:, None], axis=0)
    expert_counts = jnp.sum(all_counts * is_own[:, None], axis=0)
    picked = picked_rows[:, 0, :]
    slots = jnp.arange(48, dtype=jnp.int32)
    thirds = jnp.arange(3, dtype=jnp.int32) * 16
    pick_slot = ((frames[:, None] - own_offsets[None, :]) & 15)[:, :, None] + thirds
    pick_pos = jnp.sum(
        jnp.where(pick_slot[:, :, :, None] == slots, picked[None, :, None, :], 0), axis=3
    )
    pick_index = jnp.where(pick_slot < own_counts[None, :, None], pick_pos, -1).reshape(1, 768)
    held_slot = ((me_tok - expert_offsets) & 15)[:, None] + thirds
    held_index = jnp.where(
        held_slot < expert_counts[:, None], (expert_offsets[:, None] + held_slot) >> 4, -1
    ).reshape(1, 48)
    row_id = expert_offsets[:, None] + slots[None, :]
    back_index = jnp.where(
        slots[None, :] < expert_counts[:, None], (row_id & 15) * 16 + (row_id >> 4), -1
    ).reshape(1, 768)
    spread_index = jnp.where(slots[None, :] < own_counts[:, None], picked, -1).reshape(1, 768)

    router_own = jnp.sum(
        jnp.where((frames == me_frame)[None, :], router_weight, jnp.zeros_like(router_weight)), axis=1
    )
    router_own = router_own[None, :]
    bias_own = lax.dynamic_slice_in_dim(reduce_bias[0].reshape(16, HD), me_tok, 1, 0).reshape(HD, 1)
    reduce_turned = reduce_weight[0].T.reshape(16, HD, 288)
    expand_turned = expand_weight[0].T
    heads, reduce_turned, bias_own, back_index, spread_index, router_own = lax.optimization_barrier(
        (heads, reduce_turned, bias_own, back_index, spread_index, router_own)
    )

    picked_out, keys, values = call(
        picked_kernel,
        (shaped(768, 2 * HD), shaped(4096, 128), shaped(80, 4096)),
        "picked_attention",
        24,
        [
            pltpu.VMEM((4096, 128), BF16),
            pltpu.VMEM((80, 4096), BF16),
            pltpu.VMEM((2, 4096, TL), F32),
            pltpu.VMEM((3, 2 * HD, TL), BF16),
            pltpu.VMEM((768, 2 * HD), BF16),
            pltpu.SemaphoreType.DMA((5,)),
        ],
        in_specs=[VMEM, VMEM],
        out_specs=(ANY, ANY, ANY),
    )(pick_index, heads)

    rows = exchange(picked_out.reshape(16, 48, 2 * HD), "tok")
    attended = main_part(heads, keys, values, 0, 4)
    rows, attended = lax.optimization_barrier((rows, attended))
    normed = call(
        normed_kernel, shaped(16, 3, D), "normed", 10, [pltpu.VMEM((48, D), F32), pltpu.VMEM((48, D), F32)]
    )(rows, output_weight, *in_hbm(out_bias, mod))
    normed = exchange(normed, "frame")
    attended = main_part(heads, keys, values, 4, 4, attended)
    normed, attended = lax.optimization_barrier((normed, attended))
    rows = call(compact_kernel, shaped(16, 16, D), "compact", 6, [pltpu.VMEM((48, D), F32)])(
        normed, held_index
    )
    rows = exchange(rows, "tok")
    attended = main_part(heads, keys, values, 8, 8, attended)
    rows, attended = lax.optimization_barrier((rows, attended))
    both, gates = call(
        expert_kernel,
        (shaped(16, 2 * HD, TL), shaped(8, TL, dtype=F32)),
        "expert",
        10,
        [pltpu.VMEM((16, HD, TL), BF16), pltpu.SemaphoreType.DMA((4,))],
        in_specs=[VMEM, VMEM, VMEM, VMEM, VMEM, ANY],
        out_specs=(ANY, VMEM),
        input_output_aliases={5: 0},
    )(
        rows.reshape(TL, D), expand_bias, router_own, expand_turned, reduce_turned, *in_hbm(attended)
    )
    both = exchange(both, "tok")
    first_block = lambda *shape: pl.BlockSpec(shape, lambda i: (0,) * len(shape))
    outs = call(
        weighted_kernel,
        shaped(768, 128),
        "weighted",
        8,
        grid=(1,),
        in_specs=[
            first_block(16, HD, TL),
            first_block(8, TL),
            first_block(HD, 1),
            first_block(1, 768),
        ],
        out_specs=first_block(768, 128),
    )(both, *in_hbm(gates, bias_own, back_index))
    outs = exchange(outs.reshape(16, 48, 128), "frame")
    residual = call(residual_kernel, shaped(TL, D), "residual", 12, [pltpu.VMEM((D, TL), BF16)])(
        *in_hbm(both, stream[0], output_weight, out_bias, mod)
    )
    mixed = call(
        scatter_kernel,
        shaped(16, HD, TL),
        "scatter",
        8,
        [pltpu.VMEM((16, HD, TL), BF16), pltpu.SemaphoreType.DMA((4,))],
        in_specs=[VMEM, VMEM],
        out_specs=ANY,
    )(outs.reshape(768, 128), *in_hbm(spread_index))
    mixed = exchange(mixed, "tok")
    layer_out = call(final_kernel, shaped(TL, D), "final", 8)(
        mixed.reshape(D, TL), *in_hbm(residual, mod)
    )
    return layer_out[None]


def solution(mesh):
    return jax.shard_map(
        per_device,
        mesh=mesh,
        in_specs=(
            P("frame", "tok", None),
            P("frame", "tok", None),
            P("frame", "tok", None),
            P("frame", "tok", None),
            P("frame", None, None),
            P(),
            P(),
            P(),
            P("frame", None, "tok"),
            P("frame", "tok"),
            P("frame", "tok", None),
            P("frame", None),
            P(None, "frame"),
            P(None, "frame", None),
        ),
        out_specs=P("frame", "tok", None),
        check_vma=False,
    )
```

```python
import functools
import math

import jax
import jax.numpy as jnp
from jax import lax
from jax.experimental import pallas as pl
from jax.experimental.pallas import tpu as pltpu
from jax.sharding import PartitionSpec as P

H = 16
HD = 72
D = 1152
TL = 256
F32 = jnp.float32
BF16 = jnp.bfloat16
SCALE = 1.0 / math.sqrt(HD)


def nt(left, right):
    return lax.dot_general(left, right, (((1,), (1,)), ((), ())), preferred_element_type=F32)


def nn(left, right):
    return jnp.dot(left, right, preferred_element_type=F32)


def eye(size):
    rows = lax.broadcasted_iota(jnp.int32, (size, size), 0)
    cols = lax.broadcasted_iota(jnp.int32, (size, size), 1)
    return (rows == cols).astype(F32).astype(BF16)


def one_hot(index, width, first=0):
    lanes = lax.broadcasted_iota(jnp.int32, (index.shape[0], width), 1)
    return (lanes == index - first).astype(F32).astype(BF16)


TILES = [(w * 256, min(256, D - w * 256)) for w in range(5)]


def copy(source, target, sem):
    return pltpu.make_async_copy(source, target, sem)


def split_kernel(k_ref, v_ref, q_ref, s_ref, out_ref, in_ref, turned_ref, in_sem, out_sem):
    loads = [copy(ref, in_ref.at[i], in_sem.at[i]) for i, ref in enumerate((k_ref, v_ref, q_ref, s_ref))]
    for load in loads:
        load.start()
    stores = []
    for i, load in enumerate(loads):
        load.wait()
        for start, size in TILES:
            turned = nt(eye(size), in_ref[i, :, start : start + size])
            for h in range(H):
                low, high = max(h * HD, start), min((h + 1) * HD, start + size)
                if low < high:
                    turned_ref[i, h, low - h * HD : high - h * HD, :] = turned[
                        low - start : high - start
                    ].astype(BF16)
        stores.append(
            copy(turned_ref.at[i], out_ref.at[:, i * HD : (i + 1) * HD, :], out_sem.at[i])
        )
        stores[-1].start()
    for store in stores:
        store.wait()


def prepare(r_ref, k_ref, v_ref):
    for j in range(16):
        keys = jnp.concatenate([r_ref[j, :HD, :].astype(F32), jnp.zeros((128 - HD, TL), F32)], axis=0)
        k_ref[j * TL : (j + 1) * TL, :] = keys.T.astype(BF16)
        v_ref[:HD, j * TL : (j + 1) * TL] = r_ref[j, HD : 2 * HD, :]
        v_ref[HD:, j * TL : (j + 1) * TL] = jnp.ones((8, TL), BF16)


def score_part(q, k_ref, s_ref, j, top):
    scores = nn(k_ref[j * 512 : (j + 1) * 512, :], q)
    s_ref[j * 512 : (j + 1) * 512, :] = scores
    for b in range(64):
        part = scores[b * 8 : (b + 1) * 8]
        top = part if top is None else jnp.maximum(top, part)
    return top


def value_part(top, v_ref, s_ref, j, total):
    weights = jnp.exp((s_ref[j * TL : (j + 1) * TL, :] - top) * SCALE).astype(BF16)
    part = nn(v_ref[:, j * TL : (j + 1) * TL], weights)
    return part if total is None else total + part


def padded(q):
    return jnp.concatenate([q.astype(F32), jnp.zeros((128 - HD, TL), F32)], axis=0).astype(BF16)


def interleave(q, top, k_ref, v_ref, next_ref, s_ref):
    new_top, total = None, None
    for j in range(16):
        if q is not None and j % 2 == 0:
            new_top = score_part(q, k_ref, next_ref, j // 2, new_top)
        if top is not None:
            total = value_part(top, v_ref, s_ref, j, total)
    if q is not None:
        new_top = jnp.max(new_top, axis=0, keepdims=True)
    if top is not None:
        total = (total[:HD] / total[HD : HD + 1]).astype(BF16)
    return new_top, total


def picked_kernel(
    idx_ref, r_ref, out_ref, keys_ref, values_ref, k_ref, v_ref, s_ref, rows_ref, done_ref, sem
):
    prepare(r_ref, k_ref, v_ref)
    stores = [copy(k_ref, keys_ref, sem.at[0]), copy(v_ref, values_ref, sem.at[1])]
    for store in stores:
        store.start()
    lines = lax.broadcasted_iota(jnp.int32, (TL, TL), 0)
    for i in range(3):
        index = idx_ref[:, i * TL : (i + 1) * TL]
        rows = None
        for j in range(16):
            table = (lines == index - j * TL).astype(F32).astype(BF16)
            part = nn(r_ref[j, 2 * HD :, :], table)
            rows = part if rows is None else rows + part
        rows_ref[i] = rows.astype(BF16)
    top = None
    for i in range(4):
        q = padded(rows_ref[i, :HD, :]) if i < 3 else None
        top, done = interleave(q, top, k_ref, v_ref, s_ref.at[i % 2], s_ref.at[1 - i % 2])
        if i > 0:
            both = jnp.concatenate([done, rows_ref[i - 1, HD:, :]], axis=0)
            block = slice((i - 1) * TL, i * TL)
            done_ref[block, :] = nt(eye(TL), both).astype(BF16)
            stores.append(copy(done_ref.at[block, :], out_ref.at[block, :], sem.at[i + 1]))
            stores[-1].start()
    for store in stores:
        store.wait()


def main_kernel(steps, aliased, *refs):
    first_ref, q_ref, k_ref, v_ref = refs[:4]
    out_ref, s_ref, top_ref = refs[4 + aliased :]
    step = pl.program_id(0)

    @pl.when(step == 0)
    def _():
        top, _ = interleave(padded(first_ref[0]), None, k_ref, v_ref, s_ref.at[0], None)
        top_ref[0] = jnp.broadcast_to(top, (8, TL))

    def one(now, last):
        q = None if last else padded(q_ref[0])
        top, done = interleave(
            q, top_ref[now, 0:1, :], k_ref, v_ref, s_ref.at[1 - now], s_ref.at[now]
        )
        if not last:
            top_ref[1 - now] = jnp.broadcast_to(top, (8, TL))
        out_ref[0] = done

    for now in range(2):

        @pl.when((step < steps - 1) & (lax.rem(step, 2) == now))
        def _(now=now):
            one(now, False)

    @pl.when(step == steps - 1)
    def _():
        one((steps - 1) % 2, True)


def main_part(heads, keys, values, first, steps, before=None):
    aliased = int(before is not None)
    head_block = lambda f: pl.BlockSpec((1, HD, TL), f)
    in_specs = [
        head_block(lambda i: (first, 2, 0)),
        head_block(lambda i: (first + jnp.minimum(i + 1, steps - 1), 2, 0)),
        pl.BlockSpec((4096, 128), lambda i: (0, 0)),
        pl.BlockSpec((80, 4096), lambda i: (0, 0)),
    ] + [pl.BlockSpec(memory_space=pl.ANY)] * aliased
    return pl.pallas_call(
        functools.partial(main_kernel, steps, aliased),
        grid=(steps,),
        in_specs=in_specs,
        out_specs=head_block(lambda i: (first + i, 1, 0)),
        out_shape=shaped(16, 2 * HD, TL),
        scratch_shapes=[
            pltpu.VMEM((2, 4096, TL), F32),
            pltpu.VMEM((2, 8, TL), F32),
        ],
        input_output_aliases={4: 0} if aliased else {},
        compiler_params=pltpu.CompilerParams(vmem_limit_bytes=18 << 20),
        cost_estimate=pl.CostEstimate(
            flops=steps * 4 * 256 * 4096 * 256, transcendentals=steps * 256 * 4096, bytes_accessed=2 << 20
        ),
        name="main_attention",
    )(*in_hbm(heads, heads, keys, values, *([before] if aliased else [])))


def normed_kernel(x_ref, w_ref, b_ref, mod_ref, out_ref, att_ref, str_ref):
    for h in range(H):
        att_ref[:, h * HD : (h + 1) * HD] = x_ref[h, :, :HD].astype(F32)
        str_ref[:, h * HD : (h + 1) * HD] = x_ref[h, :, HD : 2 * HD].astype(F32)
    projected = nn(att_ref[...].astype(BF16), w_ref[...]) + b_ref[...]
    residual = (str_ref[...] + mod_ref[0:1, :] * projected).astype(BF16).astype(F32)
    centred = residual - jnp.mean(residual, axis=1, keepdims=True)
    variance = jnp.mean(centred * centred, axis=1, keepdims=True)
    normed = centred * lax.rsqrt(variance + 1e-06) * (1.0 + mod_ref[2:3, :]) + mod_ref[1:2, :]
    att_ref[...] = normed
    for e in range(16):
        out_ref[e] = att_ref[3 * e : 3 * e + 3, :].astype(BF16)


def compact_kernel(x_ref, idx_ref, out_ref, rows_ref):
    for g in range(16):
        rows_ref[3 * g : 3 * g + 3, :] = x_ref[g].astype(F32)
    lines = lax.broadcasted_iota(jnp.int32, (16, 48), 0)
    table = (lines == idx_ref[...]).astype(F32).astype(BF16)
    rows = nn(table, rows_ref[...].astype(BF16)).astype(BF16)
    for t in range(16):
        out_ref[t] = rows


def expert_kernel(x_ref, be_ref, router_ref, we_ref, wr_ref, _, out_ref, gate_ref, part_ref, sem):
    rows = x_ref[...]
    router = jnp.broadcast_to(router_ref[...].astype(F32), (8, D)).astype(BF16)
    gate_ref[...] = jax.nn.sigmoid(nt(router, rows)).astype(BF16).astype(F32)
    hidden = jax.nn.gelu(nt(rows, we_ref[...]) + be_ref[...], approximate=True).astype(BF16)
    stores = []
    for c in range(16):
        part_ref[c] = nt(wr_ref[c], hidden).astype(BF16)
        if c % 4 == 3:
            block = slice(c - 3, c + 1)
            stores.append(copy(part_ref.at[block], out_ref.at[block, :HD, :], sem.at[c // 4]))
            stores[-1].start()
    for store in stores:
        store.wait()


def weighted_kernel(x_ref, gate_ref, rb_ref, idx_ref, out_ref):
    total = x_ref[0, :HD, :].astype(F32)
    for t in range(1, 16):
        total = total + x_ref[t, :HD, :].astype(F32)
    rows = (total + rb_ref[...]).astype(BF16).astype(F32)
    rows = (rows * gate_ref[0:1, :]).astype(BF16)
    lines = lax.broadcasted_iota(jnp.int32, (TL, TL), 0)
    for i in range(3):
        block = slice(i * TL, (i + 1) * TL)
        table = (lines == idx_ref[:, block]).astype(F32).astype(BF16)
        slots = jnp.concatenate([nn(rows, table), jnp.zeros((128 - HD, TL), F32)], axis=0)
        out_ref[block, :] = nt(eye(TL), slots.astype(BF16)).astype(BF16)


def scatter_kernel(p_ref, idx_ref, out_ref, mix_ref, sem):
    turned = nt(eye(128)[:HD], p_ref[...]).astype(BF16)
    index = idx_ref[...]
    lines = lax.broadcasted_iota(jnp.int32, (TL, 768), 0)
    stores = []
    for t in range(16):
        table = (lines == index - t * TL).astype(F32).astype(BF16)
        mix_ref[t] = nt(turned, table).astype(BF16)
        if t % 4 == 3:
            block = slice(t - 3, t + 1)
            stores.append(copy(mix_ref.at[block], out_ref.at[block], sem.at[t // 4]))
            stores[-1].start()
    for store in stores:
        store.wait()


def residual_kernel(o_ref, s_ref, w_ref, b_ref, mod_ref, out_ref, att_ref):
    for h in range(H):
        att_ref[h * HD : (h + 1) * HD, :] = o_ref[h, HD:, :]
    projected = None
    for start, size in TILES:
        rows = nt(eye(TL), att_ref[start : start + size, :]).astype(BF16)
        part = nn(rows, w_ref[start : start + size, :])
        projected = part if projected is None else projected + part
    projected = projected + b_ref[...]
    out_ref[...] = (s_ref[...].astype(F32) + mod_ref[0:1, :] * projected).astype(BF16)


def final_kernel(m_ref, res_ref, mod_ref, out_ref):
    for start, size in TILES:
        cols = slice(start, start + size)
        mixed = nt(eye(TL), m_ref[cols, :])
        out_ref[:, cols] = (res_ref[:, cols].astype(F32) + mod_ref[3:4, cols] * mixed).astype(BF16)


ANY = pl.BlockSpec(memory_space=pl.ANY)
VMEM = pl.BlockSpec(memory_space=pltpu.VMEM)


def call(kernel, out_shape, name, mib, scratch=(), **specs):
    return pl.pallas_call(
        kernel,
        out_shape=out_shape,
        **specs,
        scratch_shapes=list(scratch),
        compiler_params=pltpu.CompilerParams(vmem_limit_bytes=mib << 20),
        name=name,
    )


def shaped(*shape, dtype=BF16):
    return pltpu.HBM(shape, dtype)


def in_hbm(*arrays):
    return [pltpu.with_memory_space_constraint(array, pltpu.HBM) for array in arrays]


def per_device(
    stream,
    queries,
    key_vectors,
    value_vectors,
    modulation,
    output_weight,
    output_bias,
    router_weight,
    expand_weight,
    expand_bias,
    reduce_weight,
    reduce_bias,
    counts,
    picked_rows,
):
    me_frame = lax.axis_index("frame").astype(jnp.int32)
    me_tok = lax.axis_index("tok").astype(jnp.int32)
    exchange = functools.partial(lax.all_to_all, split_axis=0, concat_axis=0, tiled=True)
    mod = modulation[0]
    out_bias = output_bias[None, :]

    sent = call(
        split_kernel,
        shaped(16, 4 * HD, TL),
        "split",
        12,
        [
            pltpu.VMEM((4, TL, D), BF16),
            pltpu.VMEM((4, 16, HD, TL), BF16),
            pltpu.SemaphoreType.DMA((4,)),
            pltpu.SemaphoreType.DMA((4,)),
        ],
        in_specs=[ANY] * 4,
        out_specs=ANY,
    )(
        *in_hbm(key_vectors[0], value_vectors[0], queries[0], stream[0])
    )
    heads = exchange(sent, "tok")

    own_counts = counts[:, 0]
    all_counts = lax.all_gather(own_counts, "frame", axis=1)
    frames = jnp.arange(16, dtype=jnp.int32)
    before = (frames[:, None] < frames[None, :]).astype(jnp.int32)
    offsets = jnp.sum(all_counts[:, :, None] * before[None, :, :], axis=1)
    is_own = (frames == me_frame).astype(jnp.int32)
    own_offsets = jnp.sum(offsets * is_own[None, :], axis=1)
    expert_offsets = jnp.sum(offsets * is_own[:, None], axis=0)
    expert_counts = jnp.sum(all_counts * is_own[:, None], axis=0)
    picked = picked_rows[:, 0, :]
    slots = jnp.arange(48, dtype=jnp.int32)
    thirds = jnp.arange(3, dtype=jnp.int32) * 16
    pick_slot = ((frames[:, None] - own_offsets[None, :]) & 15)[:, :, None] + thirds
    pick_pos = jnp.sum(
        jnp.where(pick_slot[:, :, :, None] == slots, picked[None, :, None, :], 0), axis=3
    )
    pick_index = jnp.where(pick_slot < own_counts[None, :, None], pick_pos, -1).reshape(1, 768)
    held_slot = ((me_tok - expert_offsets) & 15)[:, None] + thirds
    held_index = jnp.where(
        held_slot < expert_counts[:, None], (expert_offsets[:, None] + held_slot) >> 4, -1
    ).reshape(1, 48)

    router_own = jnp.sum(
        jnp.where((frames == me_frame)[None, :], router_weight, jnp.zeros_like(router_weight)), axis=1
    )
    router_own = router_own[None, :]
    reduce_turned = reduce_weight[0].T.reshape(16, HD, 288)
    expand_turned = expand_weight[0].T
    heads, reduce_turned, router_own = lax.optimization_barrier((heads, reduce_turned, router_own))

    picked_out, keys, values = call(
        picked_kernel,
        (shaped(768, 2 * HD), shaped(4096, 128), shaped(80, 4096)),
        "picked_attention",
        24,
        [
            pltpu.VMEM((4096, 128), BF16),
            pltpu.VMEM((80, 4096), BF16),
            pltpu.VMEM((2, 4096, TL), F32),
            pltpu.VMEM((3, 2 * HD, TL), BF16),
            pltpu.VMEM((768, 2 * HD), BF16),
            pltpu.SemaphoreType.DMA((5,)),
        ],
        in_specs=[VMEM, VMEM],
        out_specs=(ANY, ANY, ANY),
    )(pick_index, heads)

    rows = exchange(picked_out.reshape(16, 48, 2 * HD), "tok")
    attended = main_part(heads, keys, values, 0, 4)
    rows, attended = lax.optimization_barrier((rows, attended))
    normed = call(
        normed_kernel, shaped(16, 3, D), "normed", 10, [pltpu.VMEM((48, D), F32), pltpu.VMEM((48, D), F32)]
    )(rows, output_weight, *in_hbm(out_bias, mod))
    normed = exchange(normed, "frame")
    attended = main_part(heads, keys, values, 4, 4, attended)
    normed, attended = lax.optimization_barrier((normed, attended))
    rows = call(compact_kernel, shaped(16, 16, D), "compact", 6, [pltpu.VMEM((48, D), F32)])(
        normed, held_index
    )
    rows = exchange(rows, "tok")
    attended = main_part(heads, keys, values, 8, 8, attended)
    rows, attended = lax.optimization_barrier((rows, attended))
    both, gates = call(
        expert_kernel,
        (shaped(16, 2 * HD, TL), shaped(8, TL, dtype=F32)),
        "expert",
        10,
        [pltpu.VMEM((16, HD, TL), BF16), pltpu.SemaphoreType.DMA((4,))],
        in_specs=[VMEM, VMEM, VMEM, VMEM, VMEM, ANY],
        out_specs=(ANY, VMEM),
        input_output_aliases={5: 0},
    )(
        rows.reshape(TL, D), expand_bias, router_own, expand_turned, reduce_turned, *in_hbm(attended)
    )
    gates, offsets, used, own_used, own_picked, own_bias = lax.optimization_barrier(
        (gates, expert_offsets, expert_counts, own_counts, picked, reduce_bias)
    )
    row_id = offsets[:, None] + slots[None, :]
    back_index = jnp.where(
        slots[None, :] < used[:, None], (row_id & 15) * 16 + (row_id >> 4), -1
    ).reshape(1, 768)
    spread_index = jnp.where(slots[None, :] < own_used[:, None], own_picked, -1).reshape(1, 768)
    bias_own = lax.dynamic_slice_in_dim(own_bias[0].reshape(16, HD), me_tok, 1, 0).reshape(HD, 1)
    both = exchange(both, "tok")
    outs = call(
        weighted_kernel, shaped(768, 128), "weighted", 8, in_specs=[VMEM] * 4, out_specs=VMEM
    )(both, *in_hbm(gates), bias_own, back_index)
    outs = exchange(outs.reshape(16, 48, 128), "frame")
    residual = call(residual_kernel, pltpu.VMEM((TL, D), BF16), "residual", 12, [pltpu.VMEM((D, TL), BF16)])(
        *in_hbm(both, stream[0], output_weight, out_bias, mod)
    )
    mixed = call(
        scatter_kernel,
        shaped(16, HD, TL),
        "scatter",
        8,
        [pltpu.VMEM((16, HD, TL), BF16), pltpu.SemaphoreType.DMA((4,))],
        in_specs=[VMEM, VMEM],
        out_specs=ANY,
    )(outs.reshape(768, 128), *in_hbm(spread_index))
    mixed = exchange(mixed, "tok")
    layer_out = call(final_kernel, shaped(TL, D), "final", 8)(
        mixed.reshape(D, TL), residual, *in_hbm(mod)
    )
    return layer_out[None]


def solution(mesh):
    return jax.shard_map(
        per_device,
        mesh=mesh,
        in_specs=(
            P("frame", "tok", None),
            P("frame", "tok", None),
            P("frame", "tok", None),
            P("frame", "tok", None),
            P("frame", None, None),
            P(),
            P(),
            P(),
            P("frame", None, "tok"),
            P("frame", "tok"),
            P("frame", "tok", None),
            P("frame", None),
            P(None, "frame"),
            P(None, "frame", None),
        ),
        out_specs=P("frame", "tok", None),
        check_vma=False,
    )
```

```python
import functools
import math

import jax
import jax.numpy as jnp
from jax import lax
from jax.experimental import pallas as pl
from jax.experimental.pallas import tpu as pltpu
from jax.sharding import PartitionSpec as P

H = 16
HD = 72
D = 1152
TL = 256
F32 = jnp.float32
BF16 = jnp.bfloat16
EXP_SCALE = math.log2(math.e) / math.sqrt(HD)


def nt(left, right):
    return lax.dot_general(left, right, (((1,), (1,)), ((), ())), preferred_element_type=F32)


def nn(left, right):
    return jnp.dot(left, right, preferred_element_type=F32)


def eye(size):
    rows = lax.broadcasted_iota(jnp.int32, (size, size), 0)
    cols = lax.broadcasted_iota(jnp.int32, (size, size), 1)
    return (rows == cols).astype(F32).astype(BF16)


def one_hot(index, width, first=0):
    lanes = lax.broadcasted_iota(jnp.int32, (index.shape[0], width), 1)
    return (lanes == index - first).astype(F32).astype(BF16)


TILES = [(w * 256, min(256, D - w * 256)) for w in range(5)]


def copy(source, target, sem):
    return pltpu.make_async_copy(source, target, sem)


def split_kernel(k_ref, v_ref, q_ref, s_ref, out_ref, in_ref, turned_ref, in_sem, out_sem):
    loads = [copy(ref, in_ref.at[i], in_sem.at[i]) for i, ref in enumerate((k_ref, v_ref, q_ref, s_ref))]
    for load in loads:
        load.start()
    stores = []
    for i, load in enumerate(loads):
        load.wait()
        for start, size in TILES:
            turned = nt(eye(size), in_ref[i, :, start : start + size])
            for h in range(H):
                low, high = max(h * HD, start), min((h + 1) * HD, start + size)
                if low < high:
                    turned_ref[i, h, low - h * HD : high - h * HD, :] = turned[
                        low - start : high - start
                    ].astype(BF16)
        stores.append(
            copy(turned_ref.at[i], out_ref.at[:, i * HD : (i + 1) * HD, :], out_sem.at[i])
        )
        stores[-1].start()
    for store in stores:
        store.wait()


def prepare(r_ref, k_ref, v_ref):
    for j in range(16):
        keys = jnp.concatenate([r_ref[j, :HD, :].astype(F32), jnp.zeros((128 - HD, TL), F32)], axis=0)
        k_ref[j * TL : (j + 1) * TL, :] = keys.T.astype(BF16)
        v_ref[:HD, j * TL : (j + 1) * TL] = r_ref[j, HD : 2 * HD, :]
        v_ref[HD:, j * TL : (j + 1) * TL] = jnp.ones((8, TL), BF16)


def score_part(q, k_ref, s_ref, j, top):
    scores = nn(k_ref[j * 512 : (j + 1) * 512, :], q)
    s_ref[j * 512 : (j + 1) * 512, :] = scores
    for b in range(64):
        part = scores[b * 8 : (b + 1) * 8]
        top = part if top is None else jnp.maximum(top, part)
    return top


def value_part(top, v_ref, s_ref, j, total):
    weights = jnp.exp2((s_ref[j * TL : (j + 1) * TL, :] - top) * EXP_SCALE).astype(BF16)
    part = nn(v_ref[:, j * TL : (j + 1) * TL], weights)
    return part if total is None else total + part


def padded(q):
    return jnp.concatenate([q.astype(F32), jnp.zeros((128 - HD, TL), F32)], axis=0).astype(BF16)


def interleave(q, top, k_ref, v_ref, next_ref, s_ref):
    new_top, total = None, None
    for j in range(16):
        if q is not None and j % 2 == 0:
            new_top = score_part(q, k_ref, next_ref, j // 2, new_top)
        if top is not None:
            total = value_part(top, v_ref, s_ref, j, total)
    if q is not None:
        new_top = jnp.max(new_top, axis=0, keepdims=True)
    if top is not None:
        total = (total[:HD] / total[HD : HD + 1]).astype(BF16)
    return new_top, total


def picked_kernel(
    idx_ref, r_ref, out_ref, keys_ref, values_ref, k_ref, v_ref, s_ref, rows_ref, done_ref, sem
):
    prepare(r_ref, k_ref, v_ref)
    stores = [copy(k_ref, keys_ref, sem.at[0]), copy(v_ref, values_ref, sem.at[1])]
    for store in stores:
        store.start()
    lines = lax.broadcasted_iota(jnp.int32, (TL, TL), 0)
    for i in range(3):
        index = idx_ref[:, i * TL : (i + 1) * TL]
        rows = None
        for j in range(16):
            table = (lines == index - j * TL).astype(F32).astype(BF16)
            part = nn(r_ref[j, 2 * HD :, :], table)
            rows = part if rows is None else rows + part
        rows_ref[i] = rows.astype(BF16)
    top = None
    for i in range(4):
        q = padded(rows_ref[i, :HD, :]) if i < 3 else None
        top, done = interleave(q, top, k_ref, v_ref, s_ref.at[i % 2], s_ref.at[1 - i % 2])
        if i > 0:
            both = jnp.concatenate([done, rows_ref[i - 1, HD:, :]], axis=0)
            block = slice((i - 1) * TL, i * TL)
            done_ref[block, :] = nt(eye(TL), both).astype(BF16)
            stores.append(copy(done_ref.at[block, :], out_ref.at[block, :], sem.at[i + 1]))
            stores[-1].start()
    for store in stores:
        store.wait()


def main_kernel(steps, aliased, *refs):
    first_ref, q_ref, k_ref, v_ref = refs[:4]
    out_ref, s_ref, top_ref = refs[4 + aliased :]
    step = pl.program_id(0)

    @pl.when(step == 0)
    def _():
        top, _ = interleave(padded(first_ref[0]), None, k_ref, v_ref, s_ref.at[0], None)
        top_ref[0] = jnp.broadcast_to(top, (8, TL))

    def one(now, last):
        q = None if last else padded(q_ref[0])
        top, done = interleave(
            q, top_ref[now, 0:1, :], k_ref, v_ref, s_ref.at[1 - now], s_ref.at[now]
        )
        if not last:
            top_ref[1 - now] = jnp.broadcast_to(top, (8, TL))
        out_ref[0] = done

    for now in range(2):

        @pl.when((step < steps - 1) & (lax.rem(step, 2) == now))
        def _(now=now):
            one(now, False)

    @pl.when(step == steps - 1)
    def _():
        one((steps - 1) % 2, True)


def main_part(heads, keys, values, first, steps, before=None):
    aliased = int(before is not None)
    head_block = lambda f: pl.BlockSpec((1, HD, TL), f)
    in_specs = [
        head_block(lambda i: (first, 2, 0)),
        head_block(lambda i: (first + jnp.minimum(i + 1, steps - 1), 2, 0)),
        pl.BlockSpec((4096, 128), lambda i: (0, 0)),
        pl.BlockSpec((80, 4096), lambda i: (0, 0)),
    ] + [pl.BlockSpec(memory_space=pl.ANY)] * aliased
    return pl.pallas_call(
        functools.partial(main_kernel, steps, aliased),
        grid=(steps,),
        in_specs=in_specs,
        out_specs=head_block(lambda i: (first + i, 1, 0)),
        out_shape=shaped(16, 2 * HD, TL),
        scratch_shapes=[
            pltpu.VMEM((2, 4096, TL), F32),
            pltpu.VMEM((2, 8, TL), F32),
        ],
        input_output_aliases={4: 0} if aliased else {},
        compiler_params=pltpu.CompilerParams(vmem_limit_bytes=18 << 20),
        cost_estimate=pl.CostEstimate(
            flops=steps * 4 * 256 * 4096 * 256, transcendentals=steps * 256 * 4096, bytes_accessed=2 << 20
        ),
        name="main_attention",
    )(*in_hbm(heads, heads, keys, values, *([before] if aliased else [])))


def normed_kernel(x_ref, w_ref, b_ref, mod_ref, out_ref, att_ref, str_ref):
    for h in range(H):
        att_ref[:, h * HD : (h + 1) * HD] = x_ref[h, :, :HD].astype(F32)
        str_ref[:, h * HD : (h + 1) * HD] = x_ref[h, :, HD : 2 * HD].astype(F32)
    projected = nn(att_ref[...].astype(BF16), w_ref[...]) + b_ref[...]
    residual = (str_ref[...] + mod_ref[0:1, :] * projected).astype(BF16).astype(F32)
    centred = residual - jnp.mean(residual, axis=1, keepdims=True)
    variance = jnp.mean(centred * centred, axis=1, keepdims=True)
    normed = centred * lax.rsqrt(variance + 1e-06) * (1.0 + mod_ref[2:3, :]) + mod_ref[1:2, :]
    att_ref[...] = normed
    for e in range(16):
        out_ref[e] = att_ref[3 * e : 3 * e + 3, :].astype(BF16)


def compact_kernel(x_ref, idx_ref, out_ref, rows_ref):
    for g in range(16):
        rows_ref[3 * g : 3 * g + 3, :] = x_ref[g].astype(F32)
    lines = lax.broadcasted_iota(jnp.int32, (16, 48), 0)
    table = (lines == idx_ref[...]).astype(F32).astype(BF16)
    rows = nn(table, rows_ref[...].astype(BF16)).astype(BF16)
    for t in range(16):
        out_ref[t] = rows


def expert_kernel(x_ref, be_ref, router_ref, we_ref, wr_ref, _, out_ref, gate_ref, part_ref, sem):
    rows = x_ref[...]
    router = jnp.broadcast_to(router_ref[...].astype(F32), (8, D)).astype(BF16)
    gate_ref[...] = jax.nn.sigmoid(nt(router, rows)).astype(BF16).astype(F32)
    hidden = jax.nn.gelu(nt(rows, we_ref[...]) + be_ref[...], approximate=True).astype(BF16)
    stores = []
    for c in range(16):
        part_ref[c] = nt(wr_ref[c], hidden).astype(BF16)
        if c % 4 == 3:
            block = slice(c - 3, c + 1)
            stores.append(copy(part_ref.at[block], out_ref.at[block, :HD, :], sem.at[c // 4]))
            stores[-1].start()
    for store in stores:
        store.wait()


def weighted_kernel(x_ref, gate_ref, rb_ref, idx_ref, out_ref):
    total = x_ref[0, :HD, :].astype(F32)
    for t in range(1, 16):
        total = total + x_ref[t, :HD, :].astype(F32)
    rows = (total + rb_ref[...]).astype(BF16).astype(F32)
    rows = (rows * gate_ref[0:1, :]).astype(BF16)
    lines = lax.broadcasted_iota(jnp.int32, (TL, TL), 0)
    for i in range(3):
        block = slice(i * TL, (i + 1) * TL)
        table = (lines == idx_ref[:, block]).astype(F32).astype(BF16)
        slots = jnp.concatenate([nn(rows, table), jnp.zeros((128 - HD, TL), F32)], axis=0)
        out_ref[block, :] = nt(eye(TL), slots.astype(BF16)).astype(BF16)


def scatter_kernel(p_ref, idx_ref, out_ref, mix_ref, sem):
    turned = nt(eye(128)[:HD], p_ref[...]).astype(BF16)
    index = idx_ref[...]
    lines = lax.broadcasted_iota(jnp.int32, (TL, 768), 0)
    stores = []
    for t in range(16):
        table = (lines == index - t * TL).astype(F32).astype(BF16)
        mix_ref[t] = nt(turned, table).astype(BF16)
        if t % 4 == 3:
            block = slice(t - 3, t + 1)
            stores.append(copy(mix_ref.at[block], out_ref.at[block], sem.at[t // 4]))
            stores[-1].start()
    for store in stores:
        store.wait()


def residual_kernel(o_ref, s_ref, w_ref, b_ref, mod_ref, out_ref, att_ref):
    for h in range(H):
        att_ref[h * HD : (h + 1) * HD, :] = o_ref[h, HD:, :]
    projected = None
    for start, size in TILES:
        rows = nt(eye(TL), att_ref[start : start + size, :]).astype(BF16)
        part = nn(rows, w_ref[start : start + size, :])
        projected = part if projected is None else projected + part
    projected = projected + b_ref[...]
    out_ref[...] = (s_ref[...].astype(F32) + mod_ref[0:1, :] * projected).astype(BF16)


def final_kernel(m_ref, res_ref, mod_ref, out_ref):
    for start, size in TILES:
        cols = slice(start, start + size)
        mixed = nt(eye(TL), m_ref[cols, :])
        out_ref[:, cols] = (res_ref[:, cols].astype(F32) + mod_ref[3:4, cols] * mixed).astype(BF16)


ANY = pl.BlockSpec(memory_space=pl.ANY)
VMEM = pl.BlockSpec(memory_space=pltpu.VMEM)


def call(kernel, out_shape, name, mib, scratch=(), **specs):
    return pl.pallas_call(
        kernel,
        out_shape=out_shape,
        **specs,
        scratch_shapes=list(scratch),
        compiler_params=pltpu.CompilerParams(vmem_limit_bytes=mib << 20),
        name=name,
    )


def shaped(*shape, dtype=BF16):
    return pltpu.HBM(shape, dtype)


def in_hbm(*arrays):
    return [pltpu.with_memory_space_constraint(array, pltpu.HBM) for array in arrays]


def per_device(
    stream,
    queries,
    key_vectors,
    value_vectors,
    modulation,
    output_weight,
    output_bias,
    router_weight,
    expand_weight,
    expand_bias,
    reduce_weight,
    reduce_bias,
    counts,
    picked_rows,
):
    me_frame = lax.axis_index("frame").astype(jnp.int32)
    me_tok = lax.axis_index("tok").astype(jnp.int32)
    exchange = functools.partial(lax.all_to_all, split_axis=0, concat_axis=0, tiled=True)
    mod = modulation[0]
    out_bias = output_bias[None, :]

    sent = call(
        split_kernel,
        shaped(16, 4 * HD, TL),
        "split",
        12,
        [
            pltpu.VMEM((4, TL, D), BF16),
            pltpu.VMEM((4, 16, HD, TL), BF16),
            pltpu.SemaphoreType.DMA((4,)),
            pltpu.SemaphoreType.DMA((4,)),
        ],
        in_specs=[ANY] * 4,
        out_specs=ANY,
    )(
        *in_hbm(key_vectors[0], value_vectors[0], queries[0], stream[0])
    )
    heads = exchange(sent, "tok")

    own_counts = counts[:, 0]
    all_counts = lax.all_gather(own_counts, "frame", axis=1)
    frames = jnp.arange(16, dtype=jnp.int32)
    before = (frames[:, None] < frames[None, :]).astype(jnp.int32)
    offsets = jnp.sum(all_counts[:, :, None] * before[None, :, :], axis=1)
    is_own = (frames == me_frame).astype(jnp.int32)
    own_offsets = jnp.sum(offsets * is_own[None, :], axis=1)
    expert_offsets = jnp.sum(offsets * is_own[:, None], axis=0)
    expert_counts = jnp.sum(all_counts * is_own[:, None], axis=0)
    picked = picked_rows[:, 0, :]
    slots = jnp.arange(48, dtype=jnp.int32)
    thirds = jnp.arange(3, dtype=jnp.int32) * 16
    pick_slot = ((frames[:, None] - own_offsets[None, :]) & 15)[:, :, None] + thirds
    pick_pos = jnp.sum(
        jnp.where(pick_slot[:, :, :, None] == slots, picked[None, :, None, :], 0), axis=3
    )
    pick_index = jnp.where(pick_slot < own_counts[None, :, None], pick_pos, -1).reshape(1, 768)
    held_slot = ((me_tok - expert_offsets) & 15)[:, None] + thirds
    held_index = jnp.where(
        held_slot < expert_counts[:, None], (expert_offsets[:, None] + held_slot) >> 4, -1
    ).reshape(1, 48)

    router_own = jnp.sum(
        jnp.where((frames == me_frame)[None, :], router_weight, jnp.zeros_like(router_weight)), axis=1
    )
    router_own = router_own[None, :]
    reduce_turned = reduce_weight[0].T.reshape(16, HD, 288)
    expand_turned = expand_weight[0].T
    heads, reduce_turned, router_own = lax.optimization_barrier((heads, reduce_turned, router_own))

    picked_out, keys, values = call(
        picked_kernel,
        (shaped(768, 2 * HD), shaped(4096, 128), shaped(80, 4096)),
        "picked_attention",
        24,
        [
            pltpu.VMEM((4096, 128), BF16),
            pltpu.VMEM((80, 4096), BF16),
            pltpu.VMEM((2, 4096, TL), F32),
            pltpu.VMEM((3, 2 * HD, TL), BF16),
            pltpu.VMEM((768, 2 * HD), BF16),
            pltpu.SemaphoreType.DMA((5,)),
        ],
        in_specs=[VMEM, VMEM],
        out_specs=(ANY, ANY, ANY),
    )(pick_index, heads)

    rows = exchange(picked_out.reshape(16, 48, 2 * HD), "tok")
    attended = main_part(heads, keys, values, 0, 4)
    rows, attended = lax.optimization_barrier((rows, attended))
    normed = call(
        normed_kernel, shaped(16, 3, D), "normed", 10, [pltpu.VMEM((48, D), F32), pltpu.VMEM((48, D), F32)]
    )(rows, output_weight, *in_hbm(out_bias, mod))
    normed = exchange(normed, "frame")
    attended = main_part(heads, keys, values, 4, 4, attended)
    normed, attended = lax.optimization_barrier((normed, attended))
    rows = call(compact_kernel, shaped(16, 16, D), "compact", 6, [pltpu.VMEM((48, D), F32)])(
        normed, held_index
    )
    rows = exchange(rows, "tok")
    attended = main_part(heads, keys, values, 8, 8, attended)
    rows, attended = lax.optimization_barrier((rows, attended))
    both, gates = call(
        expert_kernel,
        (shaped(16, 2 * HD, TL), shaped(8, TL, dtype=F32)),
        "expert",
        10,
        [pltpu.VMEM((16, HD, TL), BF16), pltpu.SemaphoreType.DMA((4,))],
        in_specs=[VMEM, VMEM, VMEM, VMEM, VMEM, ANY],
        out_specs=(ANY, VMEM),
        input_output_aliases={5: 0},
    )(
        rows.reshape(TL, D), expand_bias, router_own, expand_turned, reduce_turned, *in_hbm(attended)
    )
    gates, offsets, used, own_used, own_picked, own_bias = lax.optimization_barrier(
        (gates, expert_offsets, expert_counts, own_counts, picked, reduce_bias)
    )
    row_id = offsets[:, None] + slots[None, :]
    back_index = jnp.where(
        slots[None, :] < used[:, None], (row_id & 15) * 16 + (row_id >> 4), -1
    ).reshape(1, 768)
    spread_index = jnp.where(slots[None, :] < own_used[:, None], own_picked, -1).reshape(1, 768)
    bias_own = lax.dynamic_slice_in_dim(own_bias[0].reshape(16, HD), me_tok, 1, 0).reshape(HD, 1)
    both = exchange(both, "tok")
    outs = call(
        weighted_kernel, shaped(768, 128), "weighted", 8, in_specs=[VMEM] * 4, out_specs=VMEM
    )(both, *in_hbm(gates), bias_own, back_index)
    outs = exchange(outs.reshape(16, 48, 128), "frame")
    residual = call(residual_kernel, pltpu.VMEM((TL, D), BF16), "residual", 12, [pltpu.VMEM((D, TL), BF16)])(
        *in_hbm(both, stream[0], output_weight, out_bias, mod)
    )
    mixed = call(
        scatter_kernel,
        shaped(16, HD, TL),
        "scatter",
        8,
        [pltpu.VMEM((16, HD, TL), BF16), pltpu.SemaphoreType.DMA((4,))],
        in_specs=[VMEM, VMEM],
        out_specs=ANY,
    )(outs.reshape(768, 128), *in_hbm(spread_index))
    mixed = exchange(mixed, "tok")
    layer_out = call(final_kernel, shaped(TL, D), "final", 8)(
        mixed.reshape(D, TL), residual, *in_hbm(mod)
    )
    return layer_out[None]


def solution(mesh):
    return jax.shard_map(
        per_device,
        mesh=mesh,
        in_specs=(
            P("frame", "tok", None),
            P("frame", "tok", None),
            P("frame", "tok", None),
            P("frame", "tok", None),
            P("frame", None, None),
            P(),
            P(),
            P(),
            P("frame", None, "tok"),
            P("frame", "tok"),
            P("frame", "tok", None),
            P("frame", None),
            P(None, "frame"),
            P(None, "frame", None),
        ),
        out_specs=P("frame", "tok", None),
        check_vma=False,
    )
```

```python
import functools
import math

import jax
import jax.numpy as jnp
from jax import lax
from jax.experimental import pallas as pl
from jax.experimental.pallas import tpu as pltpu
from jax.sharding import PartitionSpec as P

H = 16
HD = 72
D = 1152
TL = 256
F32 = jnp.float32
BF16 = jnp.bfloat16
EXP_SCALE = math.log2(math.e) / math.sqrt(HD)


def nt(left, right):
    return lax.dot_general(left, right, (((1,), (1,)), ((), ())), preferred_element_type=F32)


def nn(left, right):
    return jnp.dot(left, right, preferred_element_type=F32)


def eye(size):
    rows = lax.broadcasted_iota(jnp.int32, (size, size), 0)
    cols = lax.broadcasted_iota(jnp.int32, (size, size), 1)
    return (rows == cols).astype(F32).astype(BF16)


def one_hot(index, width, first=0):
    lanes = lax.broadcasted_iota(jnp.int32, (index.shape[0], width), 1)
    return (lanes == index - first).astype(F32).astype(BF16)


TILES = [(w * 256, min(256, D - w * 256)) for w in range(5)]


def copy(source, target, sem):
    return pltpu.make_async_copy(source, target, sem)


def split_kernel(k_ref, v_ref, q_ref, s_ref, out_ref, in_ref, turned_ref, in_sem, out_sem):
    loads = [copy(ref, in_ref.at[i], in_sem.at[i]) for i, ref in enumerate((k_ref, v_ref, q_ref, s_ref))]
    for load in loads:
        load.start()
    stores = []
    for i, load in enumerate(loads):
        load.wait()
        for start, size in TILES:
            turned = nt(eye(size), in_ref[i, :, start : start + size])
            for h in range(H):
                low, high = max(h * HD, start), min((h + 1) * HD, start + size)
                if low < high:
                    turned_ref[i, h, low - h * HD : high - h * HD, :] = turned[
                        low - start : high - start
                    ].astype(BF16)
        stores.append(
            copy(turned_ref.at[i], out_ref.at[:, i * HD : (i + 1) * HD, :], out_sem.at[i])
        )
        stores[-1].start()
    for store in stores:
        store.wait()


def prepare(r_ref, k_ref, v_ref):
    for j in range(16):
        keys = jnp.concatenate([r_ref[j, :HD, :].astype(F32), jnp.zeros((128 - HD, TL), F32)], axis=0)
        k_ref[j * TL : (j + 1) * TL, :] = keys.T.astype(BF16)
        v_ref[:HD, j * TL : (j + 1) * TL] = r_ref[j, HD : 2 * HD, :]
        v_ref[HD:, j * TL : (j + 1) * TL] = jnp.ones((8, TL), BF16)


def score_part(q, k_ref, s_ref, j, top):
    scores = nn(k_ref[j * TL : (j + 1) * TL, :], q)
    s_ref[j * TL : (j + 1) * TL, :] = scores
    for b in range(TL // 8):
        part = scores[b * 8 : (b + 1) * 8]
        top = part if top is None else jnp.maximum(top, part)
    return top


def value_part(top, v_ref, s_ref, j, total):
    weights = jnp.exp2((s_ref[j * TL : (j + 1) * TL, :] - top) * EXP_SCALE).astype(BF16)
    part = nn(v_ref[:, j * TL : (j + 1) * TL], weights)
    return part if total is None else total + part


def padded(q):
    return jnp.concatenate([q.astype(F32), jnp.zeros((128 - HD, TL), F32)], axis=0).astype(BF16)


def interleave(q, top, k_ref, v_ref, next_ref, s_ref):
    new_top, total = None, None
    for j in range(16):
        if q is not None:
            new_top = score_part(q, k_ref, next_ref, j, new_top)
        if top is not None:
            total = value_part(top, v_ref, s_ref, j, total)
    if q is not None:
        new_top = jnp.max(new_top, axis=0, keepdims=True)
    if top is not None:
        total = (total[:HD] / total[HD : HD + 1]).astype(BF16)
    return new_top, total


def picked_kernel(
    idx_ref, r_ref, out_ref, keys_ref, values_ref, k_ref, v_ref, s_ref, rows_ref, done_ref, sem
):
    prepare(r_ref, k_ref, v_ref)
    stores = [copy(k_ref, keys_ref, sem.at[0]), copy(v_ref, values_ref, sem.at[1])]
    for store in stores:
        store.start()
    lines = lax.broadcasted_iota(jnp.int32, (TL, TL), 0)
    for i in range(3):
        index = idx_ref[:, i * TL : (i + 1) * TL]
        rows = None
        for j in range(16):
            table = (lines == index - j * TL).astype(F32).astype(BF16)
            part = nn(r_ref[j, 2 * HD :, :], table)
            rows = part if rows is None else rows + part
        rows_ref[i] = rows.astype(BF16)
    top = None
    for i in range(4):
        q = padded(rows_ref[i, :HD, :]) if i < 3 else None
        top, done = interleave(q, top, k_ref, v_ref, s_ref.at[i % 2], s_ref.at[1 - i % 2])
        if i > 0:
            both = jnp.concatenate([done, rows_ref[i - 1, HD:, :]], axis=0)
            block = slice((i - 1) * TL, i * TL)
            done_ref[block, :] = nt(eye(TL), both).astype(BF16)
            stores.append(copy(done_ref.at[block, :], out_ref.at[block, :], sem.at[i + 1]))
            stores[-1].start()
    for store in stores:
        store.wait()


def main_kernel(steps, aliased, *refs):
    first_ref, q_ref, k_ref, v_ref = refs[:4]
    out_ref, s_ref, top_ref = refs[4 + aliased :]
    step = pl.program_id(0)

    @pl.when(step == 0)
    def _():
        top, _ = interleave(padded(first_ref[0]), None, k_ref, v_ref, s_ref.at[0], None)
        top_ref[0] = jnp.broadcast_to(top, (8, TL))

    def one(now, last):
        q = None if last else padded(q_ref[0])
        top, done = interleave(
            q, top_ref[now, 0:1, :], k_ref, v_ref, s_ref.at[1 - now], s_ref.at[now]
        )
        if not last:
            top_ref[1 - now] = jnp.broadcast_to(top, (8, TL))
        out_ref[0] = done

    for now in range(2):

        @pl.when((step < steps - 1) & (lax.rem(step, 2) == now))
        def _(now=now):
            one(now, False)

    @pl.when(step == steps - 1)
    def _():
        one((steps - 1) % 2, True)


def main_part(heads, keys, values, first, steps, before=None):
    aliased = int(before is not None)
    head_block = lambda f: pl.BlockSpec((1, HD, TL), f)
    in_specs = [
        head_block(lambda i: (first, 2, 0)),
        head_block(lambda i: (first + jnp.minimum(i + 1, steps - 1), 2, 0)),
        pl.BlockSpec((4096, 128), lambda i: (0, 0)),
        pl.BlockSpec((80, 4096), lambda i: (0, 0)),
    ] + [pl.BlockSpec(memory_space=pl.ANY)] * aliased
    return pl.pallas_call(
        functools.partial(main_kernel, steps, aliased),
        grid=(steps,),
        in_specs=in_specs,
        out_specs=head_block(lambda i: (first + i, 1, 0)),
        out_shape=shaped(16, 2 * HD, TL),
        scratch_shapes=[
            pltpu.VMEM((2, 4096, TL), F32),
            pltpu.VMEM((2, 8, TL), F32),
        ],
        input_output_aliases={4: 0} if aliased else {},
        compiler_params=pltpu.CompilerParams(vmem_limit_bytes=18 << 20),
        cost_estimate=pl.CostEstimate(
            flops=steps * 4 * 256 * 4096 * 256, transcendentals=steps * 256 * 4096, bytes_accessed=2 << 20
        ),
        name="main_attention",
    )(*in_hbm(heads, heads, keys, values, *([before] if aliased else [])))


def normed_kernel(x_ref, w_ref, b_ref, mod_ref, out_ref, att_ref, str_ref):
    for h in range(H):
        att_ref[:, h * HD : (h + 1) * HD] = x_ref[h, :, :HD].astype(F32)
        str_ref[:, h * HD : (h + 1) * HD] = x_ref[h, :, HD : 2 * HD].astype(F32)
    projected = nn(att_ref[...].astype(BF16), w_ref[...]) + b_ref[...]
    residual = (str_ref[...] + mod_ref[0:1, :] * projected).astype(BF16).astype(F32)
    centred = residual - jnp.mean(residual, axis=1, keepdims=True)
    variance = jnp.mean(centred * centred, axis=1, keepdims=True)
    normed = centred * lax.rsqrt(variance + 1e-06) * (1.0 + mod_ref[2:3, :]) + mod_ref[1:2, :]
    att_ref[...] = normed
    for e in range(16):
        out_ref[e] = att_ref[3 * e : 3 * e + 3, :].astype(BF16)


def compact_kernel(x_ref, idx_ref, out_ref, rows_ref):
    for g in range(16):
        rows_ref[3 * g : 3 * g + 3, :] = x_ref[g].astype(F32)
    lines = lax.broadcasted_iota(jnp.int32, (16, 48), 0)
    table = (lines == idx_ref[...]).astype(F32).astype(BF16)
    rows = nn(table, rows_ref[...].astype(BF16)).astype(BF16)
    for t in range(16):
        out_ref[t] = rows


def expert_kernel(x_ref, be_ref, router_ref, we_ref, wr_ref, _, out_ref, gate_ref, part_ref, sem):
    rows = x_ref[...]
    router = jnp.broadcast_to(router_ref[...].astype(F32), (8, D)).astype(BF16)
    gate_ref[...] = jax.nn.sigmoid(nt(router, rows)).astype(BF16).astype(F32)
    hidden = jax.nn.gelu(nt(rows, we_ref[...]) + be_ref[...], approximate=True).astype(BF16)
    stores = []
    for c in range(16):
        part_ref[c] = nt(wr_ref[c], hidden).astype(BF16)
        if c % 4 == 3:
            block = slice(c - 3, c + 1)
            stores.append(copy(part_ref.at[block], out_ref.at[block, :HD, :], sem.at[c // 4]))
            stores[-1].start()
    for store in stores:
        store.wait()


def weighted_kernel(x_ref, gate_ref, rb_ref, idx_ref, out_ref):
    total = x_ref[0, :HD, :].astype(F32)
    for t in range(1, 16):
        total = total + x_ref[t, :HD, :].astype(F32)
    rows = (total + rb_ref[...]).astype(BF16).astype(F32)
    rows = (rows * gate_ref[0:1, :]).astype(BF16)
    lines = lax.broadcasted_iota(jnp.int32, (TL, TL), 0)
    for i in range(3):
        block = slice(i * TL, (i + 1) * TL)
        table = (lines == idx_ref[:, block]).astype(F32).astype(BF16)
        slots = jnp.concatenate([nn(rows, table), jnp.zeros((128 - HD, TL), F32)], axis=0)
        out_ref[block, :] = nt(eye(TL), slots.astype(BF16)).astype(BF16)


def scatter_kernel(p_ref, idx_ref, out_ref, mix_ref, sem):
    turned = nt(eye(128)[:HD], p_ref[...]).astype(BF16)
    index = idx_ref[...]
    lines = lax.broadcasted_iota(jnp.int32, (TL, 768), 0)
    stores = []
    for t in range(16):
        table = (lines == index - t * TL).astype(F32).astype(BF16)
        mix_ref[t] = nt(turned, table).astype(BF16)
        if t % 4 == 3:
            block = slice(t - 3, t + 1)
            stores.append(copy(mix_ref.at[block], out_ref.at[block], sem.at[t // 4]))
            stores[-1].start()
    for store in stores:
        store.wait()


def residual_kernel(o_ref, s_ref, w_ref, b_ref, mod_ref, out_ref, att_ref):
    for h in range(H):
        att_ref[h * HD : (h + 1) * HD, :] = o_ref[h, HD:, :]
    projected = None
    for start, size in TILES:
        rows = nt(eye(TL), att_ref[start : start + size, :]).astype(BF16)
        part = nn(rows, w_ref[start : start + size, :])
        projected = part if projected is None else projected + part
    projected = projected + b_ref[...]
    out_ref[...] = (s_ref[...].astype(F32) + mod_ref[0:1, :] * projected).astype(BF16)


def final_kernel(m_ref, res_ref, mod_ref, out_ref):
    for start, size in TILES:
        cols = slice(start, start + size)
        mixed = nt(eye(TL), m_ref[cols, :])
        out_ref[:, cols] = (res_ref[:, cols].astype(F32) + mod_ref[3:4, cols] * mixed).astype(BF16)


ANY = pl.BlockSpec(memory_space=pl.ANY)
VMEM = pl.BlockSpec(memory_space=pltpu.VMEM)


def call(kernel, out_shape, name, mib, scratch=(), **specs):
    return pl.pallas_call(
        kernel,
        out_shape=out_shape,
        **specs,
        scratch_shapes=list(scratch),
        compiler_params=pltpu.CompilerParams(vmem_limit_bytes=mib << 20),
        name=name,
    )


def shaped(*shape, dtype=BF16):
    return pltpu.HBM(shape, dtype)


def in_hbm(*arrays):
    return [pltpu.with_memory_space_constraint(array, pltpu.HBM) for array in arrays]


def per_device(
    stream,
    queries,
    key_vectors,
    value_vectors,
    modulation,
    output_weight,
    output_bias,
    router_weight,
    expand_weight,
    expand_bias,
    reduce_weight,
    reduce_bias,
    counts,
    picked_rows,
):
    me_frame = lax.axis_index("frame").astype(jnp.int32)
    me_tok = lax.axis_index("tok").astype(jnp.int32)
    exchange = functools.partial(lax.all_to_all, split_axis=0, concat_axis=0, tiled=True)
    mod = modulation[0]
    out_bias = output_bias[None, :]

    sent = call(
        split_kernel,
        shaped(16, 4 * HD, TL),
        "split",
        12,
        [
            pltpu.VMEM((4, TL, D), BF16),
            pltpu.VMEM((4, 16, HD, TL), BF16),
            pltpu.SemaphoreType.DMA((4,)),
            pltpu.SemaphoreType.DMA((4,)),
        ],
        in_specs=[ANY] * 4,
        out_specs=ANY,
    )(
        *in_hbm(key_vectors[0], value_vectors[0], queries[0], stream[0])
    )
    heads = exchange(sent, "tok")

    own_counts = counts[:, 0]
    all_counts = lax.all_gather(own_counts, "frame", axis=1)
    frames = jnp.arange(16, dtype=jnp.int32)
    before = (frames[:, None] < frames[None, :]).astype(jnp.int32)
    offsets = jnp.sum(all_counts[:, :, None] * before[None, :, :], axis=1)
    is_own = (frames == me_frame).astype(jnp.int32)
    own_offsets = jnp.sum(offsets * is_own[None, :], axis=1)
    expert_offsets = jnp.sum(offsets * is_own[:, None], axis=0)
    expert_counts = jnp.sum(all_counts * is_own[:, None], axis=0)
    picked = picked_rows[:, 0, :]
    slots = jnp.arange(48, dtype=jnp.int32)
    thirds = jnp.arange(3, dtype=jnp.int32) * 16
    pick_slot = ((frames[:, None] - own_offsets[None, :]) & 15)[:, :, None] + thirds
    pick_pos = jnp.sum(
        jnp.where(pick_slot[:, :, :, None] == slots, picked[None, :, None, :], 0), axis=3
    )
    pick_index = jnp.where(pick_slot < own_counts[None, :, None], pick_pos, -1).reshape(1, 768)
    held_slot = ((me_tok - expert_offsets) & 15)[:, None] + thirds
    held_index = jnp.where(
        held_slot < expert_counts[:, None], (expert_offsets[:, None] + held_slot) >> 4, -1
    ).reshape(1, 48)

    router_own = jnp.sum(
        jnp.where((frames == me_frame)[None, :], router_weight, jnp.zeros_like(router_weight)), axis=1
    )
    router_own = router_own[None, :]
    reduce_turned = reduce_weight[0].T.reshape(16, HD, 288)
    expand_turned = expand_weight[0].T
    heads, reduce_turned, router_own = lax.optimization_barrier((heads, reduce_turned, router_own))

    picked_out, keys, values = call(
        picked_kernel,
        (shaped(768, 2 * HD), shaped(4096, 128), shaped(80, 4096)),
        "picked_attention",
        24,
        [
            pltpu.VMEM((4096, 128), BF16),
            pltpu.VMEM((80, 4096), BF16),
            pltpu.VMEM((2, 4096, TL), F32),
            pltpu.VMEM((3, 2 * HD, TL), BF16),
            pltpu.VMEM((768, 2 * HD), BF16),
            pltpu.SemaphoreType.DMA((5,)),
        ],
        in_specs=[VMEM, VMEM],
        out_specs=(ANY, ANY, ANY),
    )(pick_index, heads)

    rows = exchange(picked_out.reshape(16, 48, 2 * HD), "tok")
    attended = main_part(heads, keys, values, 0, 4)
    rows, attended = lax.optimization_barrier((rows, attended))
    normed = call(
        normed_kernel, shaped(16, 3, D), "normed", 10, [pltpu.VMEM((48, D), F32), pltpu.VMEM((48, D), F32)]
    )(rows, output_weight, *in_hbm(out_bias, mod))
    normed = exchange(normed, "frame")
    attended = main_part(heads, keys, values, 4, 4, attended)
    normed, attended = lax.optimization_barrier((normed, attended))
    rows = call(compact_kernel, shaped(16, 16, D), "compact", 6, [pltpu.VMEM((48, D), F32)])(
        normed, held_index
    )
    rows = exchange(rows, "tok")
    attended = main_part(heads, keys, values, 8, 8, attended)
    rows, attended = lax.optimization_barrier((rows, attended))
    both, gates = call(
        expert_kernel,
        (shaped(16, 2 * HD, TL), shaped(8, TL, dtype=F32)),
        "expert",
        10,
        [pltpu.VMEM((16, HD, TL), BF16), pltpu.SemaphoreType.DMA((4,))],
        in_specs=[VMEM, VMEM, VMEM, VMEM, VMEM, ANY],
        out_specs=(ANY, VMEM),
        input_output_aliases={5: 0},
    )(
        rows.reshape(TL, D), expand_bias, router_own, expand_turned, reduce_turned, *in_hbm(attended)
    )
    gates, offsets, used, own_used, own_picked, own_bias = lax.optimization_barrier(
        (gates, expert_offsets, expert_counts, own_counts, picked, reduce_bias)
    )
    row_id = offsets[:, None] + slots[None, :]
    back_index = jnp.where(
        slots[None, :] < used[:, None], (row_id & 15) * 16 + (row_id >> 4), -1
    ).reshape(1, 768)
    spread_index = jnp.where(slots[None, :] < own_used[:, None], own_picked, -1).reshape(1, 768)
    bias_own = lax.dynamic_slice_in_dim(own_bias[0].reshape(16, HD), me_tok, 1, 0).reshape(HD, 1)
    both = exchange(both, "tok")
    outs = call(
        weighted_kernel, shaped(768, 128), "weighted", 8, in_specs=[VMEM] * 4, out_specs=VMEM
    )(both, *in_hbm(gates), bias_own, back_index)
    outs = exchange(outs.reshape(16, 48, 128), "frame")
    residual = call(residual_kernel, pltpu.VMEM((TL, D), BF16), "residual", 12, [pltpu.VMEM((D, TL), BF16)])(
        *in_hbm(both, stream[0], output_weight, out_bias, mod)
    )
    mixed = call(
        scatter_kernel,
        shaped(16, HD, TL),
        "scatter",
        8,
        [pltpu.VMEM((16, HD, TL), BF16), pltpu.SemaphoreType.DMA((4,))],
        in_specs=[VMEM, VMEM],
        out_specs=ANY,
    )(outs.reshape(768, 128), *in_hbm(spread_index))
    mixed = exchange(mixed, "tok")
    layer_out = call(final_kernel, shaped(TL, D), "final", 8)(
        mixed.reshape(D, TL), residual, *in_hbm(mod)
    )
    return layer_out[None]


def solution(mesh):
    return jax.shard_map(
        per_device,
        mesh=mesh,
        in_specs=(
            P("frame", "tok", None),
            P("frame", "tok", None),
            P("frame", "tok", None),
            P("frame", "tok", None),
            P("frame", None, None),
            P(),
            P(),
            P(),
            P("frame", None, "tok"),
            P("frame", "tok"),
            P("frame", "tok", None),
            P("frame", None),
            P(None, "frame"),
            P(None, "frame", None),
        ),
        out_specs=P("frame", "tok", None),
        check_vma=False,
    )
```
